128 devices in a mesh: rep: 2 (over core), exp: 64 (over y, z, x).
Axes of the slice: x: 4, y: 4, z: 4, core: 2. Of those that a mesh axis runs over, the one named last changes fastest.
Arguments:
- tokens: bfloat16 [16384, 4096], P(('rep', 'exp')), may hold values from -6 to 6
- expert_ids: int32 [16384, 8], P(('rep', 'exp')), may hold values from 0 to 63, all different within a row; in each aligned block of 128 rows (0 to 127, 128 to 255, ...) at most 18 rows name the same one
- route_weights: bfloat16 [16384, 8], P(('rep', 'exp')), may hold values from 0.099609375 to 1
- cotangent: bfloat16 [16384, 4096], P(('rep', 'exp')), may hold values from -0.3984375 to 0.3984375
- w_gate: bfloat16 [64, 4096, 768], P('exp'), may hold values from -0.09375 to 0.09375
- w_up: bfloat16 [64, 4096, 768], P('exp'), may hold values from -0.09375 to 0.09375
- w_down: bfloat16 [64, 768, 4096], P('exp'), may hold values from -0.21875 to 0.21875
- ia3_scale: float32 [64, 768], P('exp'), may hold values from 0.25 to 1.75
Outputs:
- mixed: bfloat16 [16384, 4096], P(('rep', 'exp'))
- ia3_grad: float32 [64, 768], P('exp')
The draws below stay inside these ranges and needn't reach their ends.
Inputs may be any that keep to these rules, and one draw needn't show every extreme that they name: `expert_ids`: among the choices of one device's 128 tokens, no expert is named more than 18 times, a bound that some block reaches; a token names 8 different experts.
All inputs are finite; a program needn't handle non-finite values.
Results may differ from the reference program's by a relative error of at most 0.0057.
Values may be sent and summed in bfloat16 or wider, within the bound.
A program may use at most 192 MiB of HBM per device.

```python
import math
import jax
import jax.numpy as jnp
import numpy as np
from jax import lax

D = 4096
FF = 768
TOP = 8
TOK_DEV = 128
EXPERTS = 64
TOKENS = 16384
MOST = 18


def steps_of(key, shape, pieces, low, high):
    def one(position, blocks):
        steps = jax.random.uniform(jax.random.fold_in(jax.random.fold_in(key, 6), position), (blocks,), jnp.float32, low / len(pieces), high / len(pieces))
        return jnp.repeat(jnp.exp(steps), shape[position] // blocks).reshape((-1,) + (1,) * (len(shape) - position - 1))

    loudness = one(*pieces[0])
    for cut in pieces[1:]:
        loudness = loudness * one(*cut)
    return loudness


def shared_out(rng, own, number, rows, number_of, top, most, skew):
    ranking = jax.random.permutation(rng, number_of)
    packed, ordinary = load_shares(number_of, rows * top, most, skew, True), load_shares(number_of, rows * top, most, skew, False)
    places = jnp.arange(number_of)

    def named(lengths, rotation):
        used = int((lengths > 0).sum())
        fixed = max(1, used // 4)
        shifted = fixed + (places - fixed + rotation * (used - fixed)) % max(1, number_of - fixed)
        return jnp.zeros((number_of,), jnp.int32).at[ranking[jnp.where(places < fixed, places, shifted)]].set(jnp.asarray(lengths, jnp.int32))

    lengths = jnp.where(number % 4 == 0, named(packed, number // 4), named(ordinary, number - number // 4 - 1))
    mixed = jax.random.permutation(jax.random.fold_in(own, 3), number_of)
    giver, sink = mixed[0:number_of // 2 * 2:2], mixed[1:number_of // 2 * 2:2]
    margin = jnp.minimum(lengths[giver] - 1, most - lengths[sink]) // 2
    margin = jnp.where((giver == ranking[0]) | (sink == ranking[0]) | (lengths[sink] == 0), 0, jnp.maximum(margin, 0))
    shifted = jax.random.randint(jax.random.fold_in(own, 4), (number_of // 2,), 0, 1 << 20) % (margin + 1)
    lengths = lengths.at[giver].add(-shifted).at[sink].add(shifted)
    items = jnp.searchsorted(jnp.cumsum(lengths), jnp.arange(rows * top), side="right").astype(jnp.int32)
    grid = items.reshape(top, rows).T
    grid = grid[jax.random.permutation(jax.random.fold_in(own, 1), rows)]
    rotation = jax.random.randint(jax.random.fold_in(own, 2), (rows, 1), 0, top)
    return jnp.take_along_axis(grid, (jnp.arange(top)[None, :] + rotation) % top, axis=1)


def load_shares(amount, total, limit, slope, full):
    loads = [(1 << 20) // math.isqrt(rank ** slope) + 1 for rank in range(1, amount + 1)]
    largest = limit if full else min(limit, max(-(-total // amount), total * loads[0] // sum(loads)))
    least = 1 if total - largest >= amount - 1 else 0
    holding, surplus = [largest] + [least] * (amount - 1), total - largest - least * (amount - 1)
    while surplus > 0:
        candidates = [i for i in range(1, amount) if holding[i] < largest] or [i for i in range(1, amount) if holding[i] < limit]
        mass, left = sum([loads[i] for i in candidates]), surplus
        for i in candidates:
            extra = min(limit - holding[i], max(1, left * loads[i] // mass), surplus)
            holding[i] = holding[i] + extra
            surplus = surplus - extra
    return np.array(holding)


def normal_values(key, dims, scale, bound, cuts=(), kind=jnp.bfloat16):
    entries = scale * jax.random.normal(key, dims, jnp.float32)
    if cuts:
        entries = entries * steps_of(key, dims, cuts, -0.22, 0.18)
    return jnp.clip(entries, -bound, bound).astype(kind)


def setup_inputs(seed: int = 0) -> dict:
    key_list = jax.random.split(jax.random.key(seed), 9)
    tokens = normal_values(key_list[0], (TOKENS, D), 1.0, 6.0, ((0, 128),))
    expert_ids_keys = jax.random.split(jax.random.fold_in(key_list[1], 1), TOKENS // TOK_DEV)
    expert_ids_turns = jax.random.permutation(jax.random.fold_in(key_list[1], 3), TOKENS // TOK_DEV)
    expert_ids = jax.vmap(lambda own, number: shared_out(jax.random.fold_in(key_list[1], 2), own, number, TOK_DEV, EXPERTS, TOP, MOST, 1))(expert_ids_keys, expert_ids_turns).reshape((TOKENS, TOP))
    route_weights = jnp.clip(0.099609375 + 0.9003906 * jax.random.uniform(key_list[2], (TOKENS, TOP), jnp.float32) ** steps_of(key_list[2], (TOKENS, TOP), ((0, 128),), -0.2, 0.2), 0.099609375, 1.0).astype(jnp.bfloat16)
    cotangent = normal_values(key_list[3], (TOKENS, D), 0.05, 0.3984375, ((0, 128),))
    w_gate = normal_values(key_list[4], (EXPERTS, D, FF), D ** -0.5, 0.09375, ((0, 64),))
    w_up = normal_values(key_list[5], (EXPERTS, D, FF), D ** -0.5, 0.09375, ((0, 64),))
    w_down = normal_values(key_list[6], (EXPERTS, FF, D), FF ** -0.5, 0.21875, ((0, 64),))
    ia3_scale = jnp.clip(1.0 + 0.15 * jax.random.normal(key_list[7], (EXPERTS, FF), jnp.float32), 0.25, 1.75)
    return dict(tokens=tokens, expert_ids=expert_ids, route_weights=route_weights, cotangent=cotangent, w_gate=w_gate, w_up=w_up, w_down=w_down, ia3_scale=ia3_scale)


def reference(tokens, expert_ids, route_weights, cotangent, w_gate, w_up, w_down, ia3_scale):
    flat_ids = expert_ids.reshape(-1)
    flat_weights = route_weights.reshape(-1).astype(jnp.float32)
    capacity = (TOKENS // TOK_DEV) * MOST

    def per_expert(y_total, expert):
        matches = flat_ids == expert
        (chosen,) = jnp.nonzero(matches, size=capacity, fill_value=0)
        chosen = chosen.astype(jnp.int32)
        used_count = jnp.sum(matches.astype(jnp.int32))
        is_valid = (jnp.arange(capacity, dtype=jnp.int32) < used_count).astype(jnp.float32)
        token_index = (chosen // TOP).astype(jnp.int32)
        gathered = tokens[token_index]
        weight_row = flat_weights[chosen] * is_valid
        gate_pre = jnp.dot(gathered, w_gate[expert], preferred_element_type=jnp.float32)
        up_pre = jnp.dot(gathered, w_up[expert], preferred_element_type=jnp.float32)
        activated = jax.nn.silu(gate_pre) * up_pre
        hidden = (ia3_scale[expert][None, :] * activated).astype(jnp.bfloat16)
        expert_out = jnp.dot(hidden, w_down[expert], preferred_element_type=jnp.float32).astype(jnp.bfloat16)
        y_total = y_total.at[token_index].add(weight_row[:, None] * expert_out.astype(jnp.float32))
        back_proj = lax.dot_general(cotangent[token_index], w_down[expert], (((1,), (1,)), ((), ())), preferred_element_type=jnp.float32)
        grad_row = jnp.sum(weight_row[:, None] * activated * back_proj, axis=0)
        return y_total, grad_row

    start = jnp.zeros((TOKENS, D), jnp.float32)
    y_total, grads = lax.scan(per_expert, start, jnp.arange(EXPERTS, dtype=jnp.int32))
    return y_total.astype(jnp.bfloat16), grads
```

```python
import random

import jax
import jax.numpy as jnp
from jax import lax
from jax.experimental import pallas as pl
from jax.experimental.pallas import tpu as pltpu
from jax.sharding import PartitionSpec as P

MESH = pl.DeviceIdType.MESH
BF, F32 = jnp.bfloat16, jnp.float32
TOK, D, FF = 128, 4096, 768
SIDE, PLANE = 4, 16
MAIN, EXTRA, ROWS = 16, 2, 72
WIDE = 1408
OFF = (0, 1408, 2816)
COLS = (1408, 1408, 1280)
STRIDE = (16, 4, 1)
OTHER = ((1, 2), (0, 2), (0, 1))


def plane_order():
    rng = random.Random(1)
    base = [(a, b) for a in range(SIDE) for b in range(SIDE) if a or b]
    rng.shuffle(base)
    order = []
    for a, b in base:
        order += [(0, a, b), (1, b, a), (2, a, b)]
    return order


ORDER = plane_order()


def kernel(tok, cot, cc, wg_hbm, wu_hbm, wd_hbm, scale, mixed, grad, x_hbm, c_hbm, r_hbm,
           t_tok, t_cot, buf_a, buf_b, part, ids, wg, wu, wd, act, hid, stage, ext, pm, acc, gsend, grecv,
           wsem, lsem, ssem, esem, id_s, id_r, bc_s, bc_r, pl_s, pl_r, red_s, red_r, rep_s, rep_r):
    rep = lax.axis_index("rep")
    me = lax.axis_index("exp")
    c = (me // 16, (me // 4) % 4, me % 4)
    sign = 1 - 2 * rep
    own = [c[OTHER[p][0]] * SIDE + c[OTHER[p][1]] for p in range(3)]

    def axis_peer(p, d):
        v = lax.rem(c[p] + d, SIDE)
        return (rep, me + (v - c[p]) * STRIDE[p]), v

    def plane_peer(p, u, w):
        return (rep, c[p] * STRIDE[p] + u * STRIDE[OTHER[p][0]] + w * STRIDE[OTHER[p][1]])

    def near(p, a, b):
        u = lax.rem(c[OTHER[p][0]] + a + SIDE, SIDE)
        w = lax.rem(c[OTHER[p][1]] + b + SIDE, SIDE)
        return u, w

    barrier = pltpu.get_barrier_semaphore()
    greet = {}
    for p in range(3):
        for d in range(1, SIDE):
            off = [0, 0, 0]
            off[p] = d
            greet[tuple(off)] = True
    for p in range(3):
        for a in range(SIDE):
            for b in range(SIDE):
                if a or b:
                    off = [0, 0, 0]
                    off[OTHER[p][0]], off[OTHER[p][1]] = a, b
                    greet[tuple(off)] = True
    for off in greet:
        y, z, x = (lax.rem(c[i] + off[i], SIDE) for i in range(3))
        pl.semaphore_signal(barrier, inc=1, device_id=(rep, y * 16 + z * 4 + x), device_id_type=MESH)
    pl.semaphore_signal(barrier, inc=1, device_id=(1 - rep, me), device_id_type=MESH)

    weights = [pltpu.make_async_copy(s.at[0], t, wsem.at[i])
               for i, (s, t) in enumerate(((wg_hbm, wg), (wu_hbm, wu), (wd_hbm, wd)))]
    mine = []
    for p in range(3):
        cols = pl.ds(0, COLS[p])
        mine.append(pltpu.make_async_copy(cc.at[p, c[p]], ids.at[p, c[p]], lsem.at[p]))
        mine.append(pltpu.make_async_copy(tok.at[:, pl.ds(OFF[p], COLS[p])], t_tok.at[p, c[p], :, cols], lsem.at[3 + p]))
        mine.append(pltpu.make_async_copy(cot.at[:, pl.ds(OFF[p], COLS[p])], t_cot.at[p, c[p], :, cols], lsem.at[6 + p]))
    for copy in mine:
        copy.start()
    pl.semaphore_wait(barrier, len(greet) + 1)

    id_out, bc_out = [], []
    for d in (2, 1, 3):
        for p in range(3):
            peer, v = axis_peer(p, d)
            id_out.append(pltpu.make_async_remote_copy(
                cc.at[p, v], ids.at[p, c[p]], id_s.at[p, d - 1], id_r.at[p, d - 1], device_id=peer, device_id_type=MESH))
    for k, (src, dst) in enumerate(((tok, t_tok), (cot, t_cot))):
        for d in (2, 1, 3):
            for p in range(3):
                peer, _ = axis_peer(p, d)
                bc_out.append(pltpu.make_async_remote_copy(
                    src.at[:, pl.ds(OFF[p], COLS[p])], dst.at[p, c[p], :, pl.ds(0, COLS[p])],
                    bc_s.at[k, p, d - 1], bc_r.at[k, p, d - 1], device_id=peer, device_id_type=MESH))
    for copy in id_out + bc_out:
        copy.start()
    for copy in weights:
        copy.start()

    def id_in(p, d):
        v = lax.rem(c[p] - d + SIDE, SIDE)
        return pltpu.make_async_remote_copy(
            cc.at[p, v], ids.at[p, v], id_s.at[p, d - 1], id_r.at[p, d - 1],
            device_id=axis_peer(p, d)[0], device_id_type=MESH)

    def bc_in(k, p, d):
        v = lax.rem(c[p] - d + SIDE, SIDE)
        src, dst = ((tok, t_tok), (cot, t_cot))[k]
        return pltpu.make_async_remote_copy(
            src.at[:, pl.ds(OFF[p], COLS[p])], dst.at[p, v, :, pl.ds(0, COLS[p])],
            bc_s.at[k, p, d - 1], bc_r.at[k, p, d - 1], device_id=axis_peer(p, d)[0], device_id_type=MESH)

    for p in range(3):
        mine[3 * p].wait()
        for d in range(1, SIDE):
            id_in(p, d).wait_recv()

    row16 = lax.broadcasted_iota(jnp.int32, (MAIN, TOK), 0).astype(F32)
    row8 = lax.broadcasted_iota(jnp.int32, (SIDE * EXTRA, TOK), 0)

    def main_mask(p, v, weigh):
        for uw in range(PLANE):
            code = ids[p, v, 0, uw:uw + 1, :]
            hit = jnp.broadcast_to(code, (MAIN, TOK)) == row16
            value = jnp.broadcast_to(ids[p, v, 1, uw:uw + 1, :], (MAIN, TOK)) if weigh else 1.0
            pm[uw * MAIN:(uw + 1) * MAIN, :] = jnp.where(hit, value, 0.0).astype(BF)

    def extra_mask(p, v, weigh):
        slot = (row8 % EXTRA + MAIN).astype(F32)
        blocks = []
        for uw in range(PLANE):
            code = jnp.broadcast_to(ids[p, v, 0, uw:uw + 1, :], row8.shape)
            value = jnp.broadcast_to(ids[p, v, 1, uw:uw + 1, :], row8.shape) if weigh else 1.0
            blocks.append(jnp.where((code == slot) & (row8 // EXTRA == v), value, 0.0))
        return jnp.concatenate(blocks, axis=0).astype(BF)

    def pick(k, p):
        src = (t_tok, t_cot)[k]
        buf = (buf_a, buf_b)[k]
        n = COLS[p]
        ones = jnp.ones((TOK, 128), BF)
        for d in range(SIDE):
            if d == 0:
                mine[3 * p + 1 + k].wait()
            else:
                bc_in(k, p, d).wait_recv()
            v = lax.rem(c[p] - d + SIDE, SIDE)
            main_mask(p, v, False)
            rows = pl.ds(pl.multiple_of(v * MAIN, MAIN), MAIN)
            got = jnp.dot(pm[...], src[p, v, :, 0:n], preferred_element_type=F32).astype(BF)
            buf[p, :, rows, 0:n] = got.reshape(PLANE, MAIN, n)
            if k == 1 and p == 2:
                main_mask(p, v, True)
                got = jnp.dot(pm[...], ones, preferred_element_type=F32).astype(BF)
                buf[p, :, rows, n:WIDE] = got.reshape(PLANE, MAIN, WIDE - n)
        got = jnp.zeros((PLANE * SIDE * EXTRA, n), F32)
        gotw = jnp.zeros((PLANE * SIDE * EXTRA, WIDE - n), F32) if n < WIDE else None
        for v in range(SIDE):
            got += jnp.dot(extra_mask(p, v, False), src[p, v, :, 0:n], preferred_element_type=F32)
            if k == 1 and p == 2:
                gotw += jnp.dot(extra_mask(p, v, True), ones, preferred_element_type=F32)
        for uw in range(PLANE):
            buf[p, uw, SIDE * MAIN:ROWS, 0:n] = got[uw * 8:uw * 8 + 8].astype(BF)
            if k == 1 and p == 2:
                buf[p, uw, SIDE * MAIN:ROWS, n:WIDE] = gotw[uw * 8:uw * 8 + 8].astype(BF)

    def width(k, p):
        return WIDE if k == 1 else COLS[p]

    LAND = (x_hbm, c_hbm, r_hbm)
    FROM = (buf_a, buf_b, buf_a)

    def hop(k, p, u, w, land):
        n = pl.ds(0, width(k, p))
        there = u * SIDE + w
        at = there if land else own[p]
        return pltpu.make_async_remote_copy(
            FROM[k].at[p, there, :, n], LAND[k].at[p, at, :, n], pl_s.at[k, p, there], pl_r.at[k, p, at],
            device_id=plane_peer(p, u, w), device_id_type=MESH)

    def keep(k, p):
        n = pl.ds(0, width(k, p))
        return pltpu.make_async_copy(FROM[k].at[p, own[p], :, n], LAND[k].at[p, own[p], :, n], ssem.at[k, p])

    def around(p, action):
        def step(i, carry):
            u, w = near(p, i // SIDE, i % SIDE)
            action(u, w)
            return carry
        lax.fori_loop(1, PLANE, step, 0)

    for k in range(2):
        for p in range(3):
            pick(k, p)
        for p, a, b in ORDER:
            u, w = near(p, sign * a, sign * b)
            hop(k, p, u, w, False).start()
        for p in range(3):
            keep(k, p).start()

    def arrived(k, p):
        keep(k, p).wait()
        around(p, lambda u, w: hop(k, p, u, w, True).wait_recv())

    def sent(k, p):
        around(p, lambda u, w: hop(k, p, u, w, False).wait_send())

    def stage_group(k, g, slot):
        src = LAND[k]
        for q in range(PLANE):
            z, x = q // SIDE, q % SIDE
            rows = pl.ds(q * MAIN, MAIN)
            pltpu.make_async_copy(
                src.at[0, q, pl.ds(pl.multiple_of(g * MAIN, MAIN), MAIN), :],
                stage.at[slot, rows, pl.ds(OFF[0], WIDE)], esem.at[slot]).start()
            pltpu.make_async_copy(
                src.at[1, g * SIDE + x, pl.ds(z * MAIN, MAIN), :],
                stage.at[slot, rows, pl.ds(OFF[1], WIDE)], esem.at[slot]).start()
            n = width(k, 2)
            pltpu.make_async_copy(
                src.at[2, g * SIDE + z, pl.ds(x * MAIN, MAIN), pl.ds(0, n)],
                stage.at[slot, rows, pl.ds(OFF[2], n)], esem.at[slot]).start()

    def stage_wait(k, slot):
        n = pl.ds(0, OFF[2] + width(k, 2))
        pltpu.make_async_copy(stage.at[slot, :, n], stage.at[slot, :, n], esem.at[slot]).wait()

    def stage_extra(k):
        src = LAND[k]
        for p in range(3):
            for q in range(PLANE):
                pltpu.make_async_copy(
                    src.at[p, q, pl.ds(SIDE * MAIN, 8), pl.ds(0, width(k, p))],
                    ext.at[pl.ds(q * 8, 8), pl.ds(OFF[p], width(k, p))], esem.at[2]).start()
        n = pl.ds(0, OFF[2] + width(k, 2))
        pltpu.make_async_copy(ext.at[:, n], ext.at[:, n], esem.at[2]).wait()

    ra = lax.broadcasted_iota(jnp.int32, (128, 128), 0)
    rb = lax.broadcasted_iota(jnp.int32, (128, 128), 1)

    def plan_row(p, r):
        pos = (r // 32, (r // 8) % 4, (r // 2) % 4)
        return (pos[OTHER[p][0]] * 4 + pos[OTHER[p][1]]) * 8 + pos[p] * 2 + r % 2

    def to_canon(p):
        return (plan_row(p, ra) == rb).astype(F32).astype(BF)

    def from_canon(p):
        return (plan_row(p, rb) == ra).astype(F32).astype(BF)

    def extra_into_stage(k, slot):
        stage_extra(k)
        for p in range(3):
            cols = slice(OFF[p], OFF[p] + width(k, p))
            block = ext[:, cols]
            if p < 2:
                block = jnp.dot(to_canon(p), block, preferred_element_type=F32).astype(BF)
            stage[slot, 0:128, cols] = block

    def expert(slot, m, row0):
        def tile(i, carry):
            cols = pl.ds(pl.multiple_of(i * 256, 256), 256)
            gate = jnp.dot(stage[slot, 0:m, 0:D], wg[:, cols], preferred_element_type=F32)
            up = jnp.dot(stage[slot, 0:m, 0:D], wu[:, cols], preferred_element_type=F32)
            value = gate / (1.0 + jnp.exp(-gate)) * up
            act[pl.ds(row0, m), cols] = value
            hid[0:m, cols] = (scale[0:1, cols] * value).astype(BF)
            return carry
        lax.fori_loop(0, FF // 256, tile, 0)

    def down(m, p):
        return jnp.dot(hid[0:m, :], wd[:, OFF[p]:OFF[p] + COLS[p]], preferred_element_type=F32).astype(BF)

    for p in range(3):
        arrived(0, p)
    for p in range(3):
        sent(0, p)
    for copy in weights:
        copy.wait()
    stage_group(0, c[0], 0)
    extra_into_stage(0, 1)
    expert(1, 128, 1024)
    for p in range(3):
        out = down(128, p)
        if p < 2:
            out = jnp.dot(from_canon(p), out, preferred_element_type=F32).astype(BF)
        for q in range(PLANE):
            buf_a[p, q, SIDE * MAIN:ROWS, 0:COLS[p]] = out[q * 8:q * 8 + 8]

    def token_group(i, carry):
        slot = i % 2
        g = lax.rem(c[0] + sign * i + SIDE, SIDE)
        stage_wait(0, slot)

        @pl.when(i < SIDE - 1)
        def _():
            stage_group(0, lax.rem(c[0] + sign * (i + 1) + SIDE, SIDE), 1 - slot)

        expert(slot, 256, pl.multiple_of(g * 256, 256))
        out = down(256, 2)
        buf_a[2, pl.ds(g * SIDE, SIDE), 0:SIDE * MAIN, 0:COLS[2]] = out.reshape(SIDE, SIDE * MAIN, COLS[2])
        out = down(256, 1)
        for z in range(SIDE):
            for x in range(SIDE):
                r = (z * SIDE + x) * MAIN
                buf_a[1, g * SIDE + x, z * MAIN:(z + 1) * MAIN, :] = out[r:r + MAIN]
        for w in range(SIDE):
            for p in (1, 2):
                w2 = lax.rem(c[OTHER[p][1]] + w, SIDE)
                if w == 0:
                    @pl.when(i > 0)
                    def _():
                        hop(2, p, g, w2, False).start()
                else:
                    hop(2, p, g, w2, False).start()
        out = down(256, 0)
        buf_a[0, :, pl.ds(pl.multiple_of(g * MAIN, MAIN), MAIN), :] = out.reshape(PLANE, MAIN, COLS[0])
        return carry

    lax.fori_loop(0, SIDE, token_group, 0)
    for p, a, b in ORDER:
        if p == 0:
            u, w = near(p, sign * a, sign * b)
            hop(2, p, u, w, False).start()
    for p in range(3):
        keep(2, p).start()

    for p in range(3):
        arrived(1, p)

    def gradient(slot, m, row0):
        def tile(i, carry):
            cols = pl.ds(pl.multiple_of(i * 256, 256), 256)
            back = lax.dot_general(stage[slot, 0:m, 0:D], wd[cols, :], (((1,), (1,)), ((), ())),
                                   preferred_element_type=F32)
            weight = stage[slot, 0:m, D:D + 128].astype(F32)[:, 0:1]
            acc[0:1, cols] += jnp.sum(weight * act[pl.ds(row0, m), cols] * back, axis=0, keepdims=True)
            return carry
        lax.fori_loop(0, FF // 256, tile, 0)

    acc[...] = jnp.zeros_like(acc)
    stage_group(1, c[0], 0)
    extra_into_stage(1, 1)
    gradient(1, 128, 1024)

    def cot_group(i, carry):
        slot = i % 2
        g = lax.rem(c[0] + sign * i + SIDE, SIDE)
        stage_wait(1, slot)

        @pl.when(i < SIDE - 1)
        def _():
            stage_group(1, lax.rem(c[0] + sign * (i + 1) + SIDE, SIDE), 1 - slot)

        gradient(slot, 256, pl.multiple_of(g * 256, 256))
        return carry

    lax.fori_loop(0, SIDE, cot_group, 0)
    gsend[...] = acc[...]
    pair = pltpu.make_async_remote_copy(gsend, grecv, rep_s, rep_r, device_id=(1 - rep, me), device_id_type=MESH)
    pair.start()

    for p in range(3):
        sent(1, p)
    red_out = []
    for p in (2, 1, 0):
        n = COLS[p]
        arrived(2, p)
        whole = pltpu.make_async_copy(r_hbm.at[p, :, :, pl.ds(0, n)], buf_b.at[p, :, :, pl.ds(0, n)], ssem.at[1, p])
        whole.start()
        for q in range(PLANE):
            pltpu.make_async_copy(
                r_hbm.at[p, q, pl.ds(SIDE * MAIN, 8), pl.ds(0, n)],
                ext.at[pl.ds(q * 8, 8), pl.ds(OFF[p], n)], esem.at[2]).start()
        e = ext.at[:, pl.ds(OFF[p], n)]
        pltpu.make_async_copy(e, e, esem.at[2]).wait()
        whole.wait()
        for d in (1, 2, 3, 0):
            peer, v = axis_peer(p, d)
            main_mask(p, v, True)
            rows = buf_b[p, :, pl.ds(pl.multiple_of(v * MAIN, MAIN), MAIN), 0:n].reshape(PLANE * MAIN, n)
            total = lax.dot_general(pm[...], rows, (((0,), (0,)), ((), ())), preferred_element_type=F32)
            total += lax.dot_general(extra_mask(p, v, True), ext[:, OFF[p]:OFF[p] + n], (((0,), (0,)), ((), ())),
                                     preferred_element_type=F32)
            if d == 0:
                part[p, 0, :, 0:n] = total.astype(BF)
            else:
                t_tok[p, d, :, 0:n] = total.astype(BF)
                copy = pltpu.make_async_remote_copy(
                    t_tok.at[p, d, :, pl.ds(0, n)], part.at[p, d, :, pl.ds(0, n)], red_s.at[p, d - 1], red_r.at[p, d - 1],
                    device_id=peer, device_id_type=MESH)
                copy.start()
                red_out.append((p, copy))
    pair.wait()
    grad[...] = acc[0:1, :] + grecv[0:1, :]
    for p in (2, 1, 0):
        n = COLS[p]
        for q, copy in red_out:
            if q == p:
                copy.wait_recv()
        total = part[p, 0, :, 0:n].astype(F32)
        for d in range(1, SIDE):
            total += part[p, d, :, 0:n].astype(F32)
        mixed[:, OFF[p]:OFF[p] + n] = total.astype(BF)

    for p in range(3):
        sent(2, p)
    for copy in id_out + bc_out:
        copy.wait_send()
    for _, copy in red_out:
        copy.wait_send()


def shards(tokens, expert_ids, route_weights, cotangent, w_gate, w_up, w_down, ia3_scale):
    owners = 64
    ids_t = expert_ids.T
    weights_t = route_weights.T.astype(F32)
    hit = ids_t[:, None, :] == jnp.arange(owners, dtype=jnp.int32)[None, :, None]
    chosen = jnp.sum(hit.astype(F32), axis=0)
    weight = jnp.sum(jnp.where(hit, weights_t[:, None, :], 0.0), axis=0)
    earlier = jnp.arange(TOK)[:, None] < jnp.arange(TOK)[None, :]
    rank = jnp.dot(chosen.astype(BF), earlier.astype(BF), preferred_element_type=F32)
    code = jnp.where(chosen > 0, rank, 99.0)
    both = jnp.stack([code, weight]).reshape(2, 4, 4, 4, TOK)
    cc = jnp.stack([
        both.transpose(1, 0, 2, 3, 4).reshape(4, 2, 16, TOK),
        both.transpose(2, 0, 1, 3, 4).reshape(4, 2, 16, TOK),
        both.transpose(3, 0, 1, 2, 4).reshape(4, 2, 16, TOK),
    ])
    hbm = pl.BlockSpec(memory_space=pl.ANY)
    vmem = pl.BlockSpec(memory_space=pltpu.VMEM)
    land = jax.ShapeDtypeStruct((3, PLANE, ROWS, WIDE), BF)
    dma = pltpu.SemaphoreType.DMA
    out = pl.pallas_call(
        kernel,
        out_shape=[jax.ShapeDtypeStruct((TOK, D), BF), jax.ShapeDtypeStruct((1, FF), F32), land, land, land],
        in_specs=[hbm] * 6 + [vmem],
        out_specs=[vmem, vmem, hbm, hbm, hbm],
        scratch_shapes=[
            pltpu.VMEM((3, SIDE, TOK, WIDE), BF),
            pltpu.VMEM((3, SIDE, TOK, WIDE), BF),
            pltpu.VMEM((3, PLANE, ROWS, WIDE), BF),
            pltpu.VMEM((3, PLANE, ROWS, WIDE), BF),
            pltpu.VMEM((3, SIDE, TOK, WIDE), BF),
            pltpu.VMEM((3, SIDE, 2, PLANE, TOK), F32),
            pltpu.VMEM((D, FF), BF),
            pltpu.VMEM((D, FF), BF),
            pltpu.VMEM((FF, D), BF),
            pltpu.VMEM((1152, FF), F32),
            pltpu.VMEM((256, FF), BF),
            pltpu.VMEM((2, 256, D + 128), BF),
            pltpu.VMEM((128, D + 128), BF),
            pltpu.VMEM((256, TOK), BF),
            pltpu.VMEM((8, FF), F32),
            pltpu.VMEM((8, FF), F32),
            pltpu.VMEM((8, FF), F32),
            dma((3,)), dma((9,)), dma((3, 3)), dma((3,)),
            dma((3, 3)), dma((3, 3)), dma((2, 3, 3)), dma((2, 3, 3)),
            dma((3, 3, PLANE)), dma((3, 3, PLANE)), dma((3, 3)), dma((3, 3)), dma(()), dma(()),
        ],
        compiler_params=pltpu.CompilerParams(collective_id=0, has_side_effects=True, vmem_limit_bytes=67043328),
    )(tokens, cotangent, cc, w_gate, w_up, w_down, ia3_scale)
    return out[0], out[1]


def solution(mesh):
    rows = P(("rep", "exp"), None)
    weights = P("exp", None, None)
    return jax.shard_map(
        shards, mesh=mesh, in_specs=(rows, rows, rows, rows, weights, weights, weights, P("exp", None)),
        out_specs=(rows, P("exp", None)), check_vma=False)
```

```python
import jax
import jax.numpy as jnp
from jax import lax
from jax.experimental import pallas as pl
from jax.experimental.pallas import tpu as pltpu
from jax.sharding import PartitionSpec as P

MESH = pl.DeviceIdType.MESH
BF, F32 = jnp.bfloat16, jnp.float32
TOK, D, FF = 128, 4096, 768
SIDE, PLANE = 4, 16
MAIN, EXTRA, ROWS = 16, 2, 72
WIDE = 1408
OFF = (0, 1408, 2816)
COLS = (1408, 1408, 1280)
STRIDE = (16, 4, 1)
OTHER = ((1, 2), (2, 0), (0, 1))


def kernel(tok, cot, cc, wg_hbm, wu_hbm, wd_hbm, scale, mixed, grad, x_hbm, c_hbm, r_hbm, y_hbm,
           t_tok, t_cot, buf_a, buf_b, part, ids, wg, wu, wd, act, hid, stage, ext, pm, acc, gsend, grecv,
           wsem, lsem, ssem, esem, id_s, id_r, bc_s, bc_r, pl_s, pl_r, y_s, y_r, red_s, red_r, rep_s, rep_r):
    rep = lax.axis_index("rep")
    me = lax.axis_index("exp")
    c = (me // 16, (me // 4) % 4, me % 4)
    own = [c[OTHER[p][0]] * SIDE + c[OTHER[p][1]] for p in range(3)]

    def axis_peer(p, d):
        v = lax.rem(c[p] + d, SIDE)
        return (rep, me + (v - c[p]) * STRIDE[p]), v

    def plane_peer(p, u, w):
        return (rep, c[p] * STRIDE[p] + u * STRIDE[OTHER[p][0]] + w * STRIDE[OTHER[p][1]])

    def near(p, a, b):
        return lax.rem(c[OTHER[p][0]] + a + SIDE, SIDE), lax.rem(c[OTHER[p][1]] + b + SIDE, SIDE)

    barrier = pltpu.get_barrier_semaphore()
    greet = [tuple(d if i == p else 0 for i in range(3)) for p in range(3) for d in range(1, SIDE)]
    for off in greet:
        y, z, x = (lax.rem(c[i] + off[i], SIDE) for i in range(3))
        pl.semaphore_signal(barrier, inc=1, device_id=(rep, y * 16 + z * 4 + x), device_id_type=MESH)
    pl.semaphore_signal(barrier, inc=1, device_id=(1 - rep, me), device_id_type=MESH)

    weights = [pltpu.make_async_copy(s.at[0], t, wsem.at[i])
               for i, (s, t) in enumerate(((wg_hbm, wg), (wu_hbm, wu), (wd_hbm, wd)))]
    mine = []
    for p in range(3):
        cols = pl.ds(0, COLS[p])
        mine.append(pltpu.make_async_copy(cc.at[p, c[p]], ids.at[p, c[p]], lsem.at[p]))
        mine.append(pltpu.make_async_copy(tok.at[:, pl.ds(OFF[p], COLS[p])], t_tok.at[p, c[p], :, cols], lsem.at[3 + p]))
        mine.append(pltpu.make_async_copy(cot.at[:, pl.ds(OFF[p], COLS[p])], t_cot.at[p, c[p], :, cols], lsem.at[6 + p]))
    for copy in mine:
        copy.start()
    pl.semaphore_wait(barrier, len(greet) + 1)

    id_out, bc_out = [], []
    for d in (2, 1, 3):
        for p in range(3):
            peer, v = axis_peer(p, d)
            id_out.append(pltpu.make_async_remote_copy(
                cc.at[p, v], ids.at[p, c[p]], id_s.at[p, d - 1], id_r.at[p, d - 1], device_id=peer, device_id_type=MESH))
    for k, (src, dst) in enumerate(((tok, t_tok), (cot, t_cot))):
        for d in (2, 1, 3):
            for p in range(3):
                peer, _ = axis_peer(p, d)
                bc_out.append(pltpu.make_async_remote_copy(
                    src.at[:, pl.ds(OFF[p], COLS[p])], dst.at[p, c[p], :, pl.ds(0, COLS[p])],
                    bc_s.at[k, p, d - 1], bc_r.at[k, p, d - 1], device_id=peer, device_id_type=MESH))
    for copy in id_out + bc_out:
        copy.start()
    for copy in weights:
        copy.start()

    def id_in(p, d):
        v = lax.rem(c[p] - d + SIDE, SIDE)
        return pltpu.make_async_remote_copy(
            cc.at[p, v], ids.at[p, v], id_s.at[p, d - 1], id_r.at[p, d - 1],
            device_id=axis_peer(p, d)[0], device_id_type=MESH)

    def bc_in(k, p, d):
        v = lax.rem(c[p] - d + SIDE, SIDE)
        src, dst = ((tok, t_tok), (cot, t_cot))[k]
        return pltpu.make_async_remote_copy(
            src.at[:, pl.ds(OFF[p], COLS[p])], dst.at[p, v, :, pl.ds(0, COLS[p])],
            bc_s.at[k, p, d - 1], bc_r.at[k, p, d - 1], device_id=axis_peer(p, d)[0], device_id_type=MESH)

    for p in range(3):
        mine[3 * p].wait()
        for d in range(1, SIDE):
            id_in(p, d).wait_recv()

    row16 = lax.broadcasted_iota(jnp.int32, (MAIN, TOK), 0).astype(F32)
    row8 = lax.broadcasted_iota(jnp.int32, (SIDE * EXTRA, TOK), 0)

    def main_mask(p, v, weigh):
        for uw in range(PLANE):
            code = ids[p, v, 0, uw:uw + 1, :]
            hit = jnp.broadcast_to(code, (MAIN, TOK)) == row16
            value = jnp.broadcast_to(ids[p, v, 1, uw:uw + 1, :], (MAIN, TOK)) if weigh else 1.0
            pm[uw * MAIN:(uw + 1) * MAIN, :] = jnp.where(hit, value, 0.0).astype(BF)

    def extra_mask(p, v, weigh):
        slot = (row8 % EXTRA + MAIN).astype(F32)
        blocks = []
        for uw in range(PLANE):
            code = jnp.broadcast_to(ids[p, v, 0, uw:uw + 1, :], row8.shape)
            value = jnp.broadcast_to(ids[p, v, 1, uw:uw + 1, :], row8.shape) if weigh else 1.0
            blocks.append(jnp.where((code == slot) & (row8 // EXTRA == v), value, 0.0))
        return jnp.concatenate(blocks, axis=0).astype(BF)

    def pick(k, p):
        src = (t_tok, t_cot)[k]
        buf = (buf_a, buf_b)[k]
        n = COLS[p]
        ones = jnp.ones((TOK, 128), BF)
        for d in range(SIDE):
            if d == 0:
                mine[3 * p + 1 + k].wait()
            else:
                bc_in(k, p, d).wait_recv()
            v = lax.rem(c[p] - d + SIDE, SIDE)
            main_mask(p, v, False)
            rows = pl.ds(pl.multiple_of(v * MAIN, MAIN), MAIN)
            got = jnp.dot(pm[...], src[p, v, :, 0:n], preferred_element_type=F32).astype(BF)
            buf[p, :, rows, 0:n] = got.reshape(PLANE, MAIN, n)
            if k == 1 and p == 2:
                main_mask(p, v, True)
                got = jnp.dot(pm[...], ones, preferred_element_type=F32).astype(BF)
                buf[p, :, rows, n:WIDE] = got.reshape(PLANE, MAIN, WIDE - n)
        got = jnp.zeros((PLANE * SIDE * EXTRA, n), F32)
        gotw = jnp.zeros((PLANE * SIDE * EXTRA, WIDE - n), F32) if n < WIDE else None
        for v in range(SIDE):
            got += jnp.dot(extra_mask(p, v, False), src[p, v, :, 0:n], preferred_element_type=F32)
            if k == 1 and p == 2:
                gotw += jnp.dot(extra_mask(p, v, True), ones, preferred_element_type=F32)
        for uw in range(PLANE):
            buf[p, uw, SIDE * MAIN:ROWS, 0:n] = got[uw * 8:uw * 8 + 8].astype(BF)
            if k == 1 and p == 2:
                buf[p, uw, SIDE * MAIN:ROWS, n:WIDE] = gotw[uw * 8:uw * 8 + 8].astype(BF)

    def width(k, p):
        return WIDE if k == 1 else COLS[p]

    LAND = (x_hbm, c_hbm, r_hbm)
    FROM = (buf_a, buf_b, buf_a)

    def hop(k, p, a, b, first):
        n = pl.ds(0, width(k, p))
        u, w = near(p, a, b)
        src = FROM[k].at[p, u * SIDE + w, :, n]
        if first:
            i = (a - 1) * 3 + b - 1
            dst, sem, to = y_hbm.at[k, p, i, :, n], y_r.at[k, p, i], plane_peer(p, u, c[OTHER[p][1]])
        else:
            dst, sem, to = LAND[k].at[p, own[p], :, n], pl_r.at[k, p, a * SIDE + b], plane_peer(p, u, w)
        return pltpu.make_async_remote_copy(
            src, dst, pl_s.at[k, p, a * SIDE + b], sem, device_id=to, device_id_type=MESH)

    def relay(k, p, a, b):
        n = pl.ds(0, width(k, p))
        i = (a - 1) * 3 + b - 1
        u, _ = near(p, -a, 0)
        _, w = near(p, 0, b)
        block = y_hbm.at[k, p, i, :, n]
        to = plane_peer(p, c[OTHER[p][0]], w)
        pltpu.make_async_remote_copy(block, block, y_s.at[k, p, i], y_r.at[k, p, i],
                                     device_id=to, device_id_type=MESH).wait_recv()
        relay_copy(k, p, a, b, u, to).start()

    def relay_copy(k, p, a, b, u, to):
        n = pl.ds(0, width(k, p))
        i = (a - 1) * 3 + b - 1
        return pltpu.make_async_remote_copy(
            y_hbm.at[k, p, i, :, n], LAND[k].at[p, u * SIDE + c[OTHER[p][1]], :, n],
            y_s.at[k, p, i], pl_r.at[k, p, a * SIDE + b], device_id=to, device_id_type=MESH)

    def relays(k, start, stop):
        def step(i, carry):
            for p in range(3):
                relay(k, p, i // 3 + 1, i % 3 + 1)
            return carry
        lax.fori_loop(start, stop, step, 0)

    def keep(k, p):
        n = pl.ds(0, width(k, p))
        return pltpu.make_async_copy(FROM[k].at[p, own[p], :, n], LAND[k].at[p, own[p], :, n], ssem.at[k, p])

    def launch(k):
        for i in range(9):
            for p in range(3):
                hop(k, p, i // 3 + 1, i % 3 + 1, True).start()
        for a in (2, 1, 3):
            for p in range(3):
                hop(k, p, 0, a, False).start()
                hop(k, p, a, 0, False).start()
        for p in range(3):
            keep(k, p).start()

    for p in range(3):
        pick(0, p)
    launch(0)
    for p in range(3):
        pick(1, p)
    relays(0, 0, 9)
    launch(1)

    def arrived(k, p):
        keep(k, p).wait()

        def step(i, carry):
            n = pl.ds(0, width(k, p))
            u, w = near(p, -(i // SIDE), -(i % SIDE))
            block = LAND[k].at[p, u * SIDE + w, :, n]
            pltpu.make_async_remote_copy(block, block, pl_s.at[k, p, i], pl_r.at[k, p, i],
                                         device_id=plane_peer(p, u, w), device_id_type=MESH).wait_recv()
            return carry
        lax.fori_loop(1, PLANE, step, 0)

    def sent(k, p):
        def step(i, carry):
            n = pl.ds(0, width(k, p))
            u, w = near(p, i // SIDE, i % SIDE)
            block = FROM[k].at[p, u * SIDE + w, :, n]
            pltpu.make_async_remote_copy(block, block, pl_s.at[k, p, i], pl_r.at[k, p, i],
                                         device_id=plane_peer(p, u, w), device_id_type=MESH).wait_send()
            return carry
        lax.fori_loop(1, PLANE, step, 0)

    def relayed(k, p):
        def step(i, carry):
            a, b = i // 3 + 1, i % 3 + 1
            u, _ = near(p, -a, 0)
            _, w = near(p, 0, b)
            relay_copy(k, p, a, b, u, plane_peer(p, c[OTHER[p][0]], w)).wait_send()
            return carry
        lax.fori_loop(0, 9, step, 0)

    def stage_group(k, g, slot):
        src = LAND[k]
        for q in range(PLANE):
            z, x = q // SIDE, q % SIDE
            rows = pl.ds(q * MAIN, MAIN)
            pltpu.make_async_copy(
                src.at[0, q, pl.ds(pl.multiple_of(g * MAIN, MAIN), MAIN), :],
                stage.at[slot, rows, pl.ds(OFF[0], WIDE)], esem.at[slot]).start()
            pltpu.make_async_copy(
                src.at[1, x * SIDE + g, pl.ds(z * MAIN, MAIN), :],
                stage.at[slot, rows, pl.ds(OFF[1], WIDE)], esem.at[slot]).start()
            n = width(k, 2)
            pltpu.make_async_copy(
                src.at[2, g * SIDE + z, pl.ds(x * MAIN, MAIN), pl.ds(0, n)],
                stage.at[slot, rows, pl.ds(OFF[2], n)], esem.at[slot]).start()

    def stage_wait(k, slot):
        n = pl.ds(0, OFF[2] + width(k, 2))
        pltpu.make_async_copy(stage.at[slot, :, n], stage.at[slot, :, n], esem.at[slot]).wait()

    def stage_extra(k):
        src = LAND[k]
        for p in range(3):
            for q in range(PLANE):
                pltpu.make_async_copy(
                    src.at[p, q, pl.ds(SIDE * MAIN, 8), pl.ds(0, width(k, p))],
                    ext.at[pl.ds(q * 8, 8), pl.ds(OFF[p], width(k, p))], esem.at[2]).start()
        n = pl.ds(0, OFF[2] + width(k, 2))
        pltpu.make_async_copy(ext.at[:, n], ext.at[:, n], esem.at[2]).wait()

    ra = lax.broadcasted_iota(jnp.int32, (128, 128), 0)
    rb = lax.broadcasted_iota(jnp.int32, (128, 128), 1)

    def plan_row(p, r):
        pos = (r // 32, (r // 8) % 4, (r // 2) % 4)
        return (pos[OTHER[p][0]] * 4 + pos[OTHER[p][1]]) * 8 + pos[p] * 2 + r % 2

    def to_canon(p):
        return (plan_row(p, ra) == rb).astype(F32).astype(BF)

    def from_canon(p):
        return (plan_row(p, rb) == ra).astype(F32).astype(BF)

    def extra_into_stage(k, slot):
        stage_extra(k)
        for p in range(3):
            cols = slice(OFF[p], OFF[p] + width(k, p))
            block = ext[:, cols]
            if p < 2:
                block = jnp.dot(to_canon(p), block, preferred_element_type=F32).astype(BF)
            stage[slot, 0:128, cols] = block

    def expert(slot, m, row0):
        def tile(i, carry):
            cols = pl.ds(pl.multiple_of(i * 256, 256), 256)
            gate = jnp.dot(stage[slot, 0:m, 0:D], wg[:, cols], preferred_element_type=F32)
            up = jnp.dot(stage[slot, 0:m, 0:D], wu[:, cols], preferred_element_type=F32)
            value = gate / (1.0 + jnp.exp(-gate)) * up
            act[pl.ds(row0, m), cols] = value
            hid[0:m, cols] = (scale[0:1, cols] * value).astype(BF)
            return carry
        lax.fori_loop(0, FF // 256, tile, 0)

    def down(m, p):
        return jnp.dot(hid[0:m, :], wd[:, OFF[p]:OFF[p] + COLS[p]], preferred_element_type=F32).astype(BF)

    for p in range(3):
        arrived(0, p)
    for p in range(3):
        sent(0, p)
    for copy in weights:
        copy.wait()
    stage_group(0, c[0], 0)
    extra_into_stage(0, 1)
    expert(1, 128, 1024)
    for p in range(3):
        out = down(128, p)
        if p < 2:
            out = jnp.dot(from_canon(p), out, preferred_element_type=F32).astype(BF)
        for q in range(PLANE):
            buf_a[p, q, SIDE * MAIN:ROWS, 0:COLS[p]] = out[q * 8:q * 8 + 8]

    def token_group(i, carry):
        slot = i % 2
        g = lax.rem(c[0] + i + SIDE, SIDE)
        stage_wait(0, slot)

        @pl.when(i < SIDE - 1)
        def _():
            stage_group(0, lax.rem(c[0] + i + 1 + SIDE, SIDE), 1 - slot)

        expert(slot, 256, pl.multiple_of(g * 256, 256))
        out = down(256, 2)
        buf_a[2, pl.ds(g * SIDE, SIDE), 0:SIDE * MAIN, 0:COLS[2]] = out.reshape(SIDE, SIDE * MAIN, COLS[2])
        out = down(256, 1)
        for z in range(SIDE):
            for x in range(SIDE):
                r = (z * SIDE + x) * MAIN
                buf_a[1, x * SIDE + g, z * MAIN:(z + 1) * MAIN, :] = out[r:r + MAIN]
        @pl.when(i == 0)
        def _():
            for a in (2, 1, 3):
                hop(2, 1, a, 0, False).start()
                hop(2, 2, 0, a, False).start()

        @pl.when(i > 0)
        def _():
            for a in (1, 2, 3):
                hop(2, 1, a, i, True).start()
                hop(2, 2, i, a, True).start()
            hop(2, 1, 0, i, False).start()
            hop(2, 2, i, 0, False).start()

        out = down(256, 0)
        buf_a[0, :, pl.ds(pl.multiple_of(g * MAIN, MAIN), MAIN), :] = out.reshape(PLANE, MAIN, COLS[0])
        relays(1, 2 * i, 2 * i + 2)
        return carry

    lax.fori_loop(0, SIDE, token_group, 0)
    for i in range(9):
        hop(2, 0, i // 3 + 1, i % 3 + 1, True).start()
    for a in (2, 1, 3):
        hop(2, 0, 0, a, False).start()
        hop(2, 0, a, 0, False).start()
    for p in range(3):
        keep(2, p).start()
    relays(1, 8, 9)

    def relay_returns(i, carry):
        for a in (1, 2, 3):
            relay(2, 1, a, i)
            relay(2, 2, i, a)
        return carry

    lax.fori_loop(1, SIDE, relay_returns, 0)

    def relay_last(i, carry):
        relay(2, 0, i // 3 + 1, i % 3 + 1)
        return carry

    lax.fori_loop(0, 9, relay_last, 0)

    for p in range(3):
        arrived(1, p)

    def gradient(slot, m, row0):
        def tile(i, carry):
            cols = pl.ds(pl.multiple_of(i * 256, 256), 256)
            back = lax.dot_general(stage[slot, 0:m, 0:D], wd[cols, :], (((1,), (1,)), ((), ())),
                                   preferred_element_type=F32)
            weight = stage[slot, 0:m, D:D + 128].astype(F32)[:, 0:1]
            acc[0:1, cols] += jnp.sum(weight * act[pl.ds(row0, m), cols] * back, axis=0, keepdims=True)
            return carry
        lax.fori_loop(0, FF // 256, tile, 0)

    acc[...] = jnp.zeros_like(acc)
    stage_group(1, c[0], 0)
    extra_into_stage(1, 1)
    gradient(1, 128, 1024)

    def cot_group(i, carry):
        slot = i % 2
        g = lax.rem(c[0] + i + SIDE, SIDE)
        stage_wait(1, slot)

        @pl.when(i < SIDE - 1)
        def _():
            stage_group(1, lax.rem(c[0] + i + 1 + SIDE, SIDE), 1 - slot)

        gradient(slot, 256, pl.multiple_of(g * 256, 256))
        return carry

    lax.fori_loop(0, SIDE, cot_group, 0)
    gsend[...] = acc[...]
    pair = pltpu.make_async_remote_copy(gsend, grecv, rep_s, rep_r, device_id=(1 - rep, me), device_id_type=MESH)
    pair.start()

    for p in range(3):
        sent(1, p)
    red_out = []
    for p in (2, 1, 0):
        n = COLS[p]
        arrived(2, p)
        whole = pltpu.make_async_copy(r_hbm.at[p, :, :, pl.ds(0, n)], buf_b.at[p, :, :, pl.ds(0, n)], ssem.at[1, p])
        whole.start()
        for q in range(PLANE):
            pltpu.make_async_copy(
                r_hbm.at[p, q, pl.ds(SIDE * MAIN, 8), pl.ds(0, n)],
                ext.at[pl.ds(q * 8, 8), pl.ds(OFF[p], n)], esem.at[2]).start()
        e = ext.at[:, pl.ds(OFF[p], n)]
        pltpu.make_async_copy(e, e, esem.at[2]).wait()
        whole.wait()
        for d in (1, 2, 3, 0):
            peer, v = axis_peer(p, d)
            main_mask(p, v, True)
            rows = buf_b[p, :, pl.ds(pl.multiple_of(v * MAIN, MAIN), MAIN), 0:n].reshape(PLANE * MAIN, n)
            total = lax.dot_general(pm[...], rows, (((0,), (0,)), ((), ())), preferred_element_type=F32)
            total += lax.dot_general(extra_mask(p, v, True), ext[:, OFF[p]:OFF[p] + n], (((0,), (0,)), ((), ())),
                                     preferred_element_type=F32)
            if d == 0:
                part[p, 0, :, 0:n] = total.astype(BF)
            else:
                t_tok[p, d, :, 0:n] = total.astype(BF)
                copy = pltpu.make_async_remote_copy(
                    t_tok.at[p, d, :, pl.ds(0, n)], part.at[p, d, :, pl.ds(0, n)], red_s.at[p, d - 1], red_r.at[p, d - 1],
                    device_id=peer, device_id_type=MESH)
                copy.start()
                red_out.append((p, copy))
    pair.wait()
    grad[...] = acc[0:1, :] + grecv[0:1, :]
    for p in (2, 1, 0):
        n = COLS[p]
        for q, copy in red_out:
            if q == p:
                copy.wait_recv()
        total = part[p, 0, :, 0:n].astype(F32)
        for d in range(1, SIDE):
            total += part[p, d, :, 0:n].astype(F32)
        mixed[:, OFF[p]:OFF[p] + n] = total.astype(BF)

    for p in range(3):
        sent(2, p)
        for k in range(3):
            relayed(k, p)
    for copy in id_out + bc_out:
        copy.wait_send()
    for _, copy in red_out:
        copy.wait_send()


def shards(tokens, expert_ids, route_weights, cotangent, w_gate, w_up, w_down, ia3_scale):
    owners = 64
    ids_t = expert_ids.T
    weights_t = route_weights.T.astype(F32)
    hit = ids_t[:, None, :] == jnp.arange(owners, dtype=jnp.int32)[None, :, None]
    chosen = jnp.sum(hit.astype(F32), axis=0)
    weight = jnp.sum(jnp.where(hit, weights_t[:, None, :], 0.0), axis=0)
    earlier = jnp.arange(TOK)[:, None] < jnp.arange(TOK)[None, :]
    rank = jnp.dot(chosen.astype(BF), earlier.astype(BF), preferred_element_type=F32)
    code = jnp.where(chosen > 0, rank, 99.0)
    both = jnp.stack([code, weight]).reshape(2, 4, 4, 4, TOK)
    cc = jnp.stack([
        both.transpose(1, 0, 2, 3, 4).reshape(4, 2, 16, TOK),
        both.transpose(2, 0, 3, 1, 4).reshape(4, 2, 16, TOK),
        both.transpose(3, 0, 1, 2, 4).reshape(4, 2, 16, TOK),
    ])
    hbm = pl.BlockSpec(memory_space=pl.ANY)
    vmem = pl.BlockSpec(memory_space=pltpu.VMEM)
    land = jax.ShapeDtypeStruct((3, PLANE, ROWS, WIDE), BF)
    dma = pltpu.SemaphoreType.DMA
    out = pl.pallas_call(
        kernel,
        out_shape=[jax.ShapeDtypeStruct((TOK, D), BF), jax.ShapeDtypeStruct((1, FF), F32), land, land, land,
                   jax.ShapeDtypeStruct((3, 3, 9, ROWS, WIDE), BF)],
        in_specs=[hbm] * 6 + [vmem],
        out_specs=[vmem, vmem, hbm, hbm, hbm, hbm],
        scratch_shapes=[
            pltpu.VMEM((3, SIDE, TOK, WIDE), BF),
            pltpu.VMEM((3, SIDE, TOK, WIDE), BF),
            pltpu.VMEM((3, PLANE, ROWS, WIDE), BF),
            pltpu.VMEM((3, PLANE, ROWS, WIDE), BF),
            pltpu.VMEM((3, SIDE, TOK, WIDE), BF),
            pltpu.VMEM((3, SIDE, 2, PLANE, TOK), F32),
            pltpu.VMEM((D, FF), BF),
            pltpu.VMEM((D, FF), BF),
            pltpu.VMEM((FF, D), BF),
            pltpu.VMEM((1152, FF), F32),
            pltpu.VMEM((256, FF), BF),
            pltpu.VMEM((2, 256, D + 128), BF),
            pltpu.VMEM((128, D + 128), BF),
            pltpu.VMEM((256, TOK), BF),
            pltpu.VMEM((8, FF), F32),
            pltpu.VMEM((8, FF), F32),
            pltpu.VMEM((8, FF), F32),
            dma((3,)), dma((9,)), dma((3, 3)), dma((3,)),
            dma((3, 3)), dma((3, 3)), dma((2, 3, 3)), dma((2, 3, 3)),
            dma((3, 3, PLANE)), dma((3, 3, PLANE)), dma((3, 3, 9)), dma((3, 3, 9)), dma((3, 3)), dma((3, 3)), dma(()), dma(()),
        ],
        compiler_params=pltpu.CompilerParams(collective_id=0, has_side_effects=True, vmem_limit_bytes=67043328),
    )(tokens, cotangent, cc, w_gate, w_up, w_down, ia3_scale)
    return out[0], out[1]


def solution(mesh):
    rows = P(("rep", "exp"), None)
    weights = P("exp", None, None)
    return jax.shard_map(
        shards, mesh=mesh, in_specs=(rows, rows, rows, rows, weights, weights, weights, P("exp", None)),
        out_specs=(rows, P("exp", None)), check_vma=False)
```

```python
import jax
import jax.numpy as jnp
from jax import lax
from jax.experimental import pallas as pl
from jax.experimental.pallas import tpu as pltpu
from jax.sharding import PartitionSpec as P

MESH = pl.DeviceIdType.MESH
BF, F32 = jnp.bfloat16, jnp.float32
TOK, D, FF = 128, 4096, 768
SIDE, PLANE = 4, 16
MAIN, EXTRA, ROWS = 16, 2, 72
WIDE = 1408
OFF = (0, 1408, 2816)
COLS = (1408, 1408, 1280)
STRIDE = (16, 4, 1)
OTHER = ((1, 2), (2, 0), (0, 1))


def kernel(tok, cot, cc, wg_hbm, wu_hbm, wd_hbm, scale, part, grad, x_hbm, c_hbm, r_hbm, y_hbm,
           t_tok, t_cot, buf_a, buf_b, r_last, ids, wg, wu, wd, act, hid, stage, ext, pm, acc, gsend, grecv,
           wsem, lsem, ssem, esem, id_s, id_r, bc_s, bc_r, hf_s, hf_r, pl_s, pl_r, y_s, y_r, red_s, red_r, rep_s, rep_r):
    rep = lax.axis_index("rep")
    me = lax.axis_index("exp")
    c = (me // 16, (me // 4) % 4, me % 4)
    own = [c[OTHER[p][0]] * SIDE + c[OTHER[p][1]] for p in range(3)]

    def axis_peer(p, d):
        v = lax.rem(c[p] + d, SIDE)
        return (rep, me + (v - c[p]) * STRIDE[p]), v

    def plane_peer(p, u, w):
        return (rep, c[p] * STRIDE[p] + u * STRIDE[OTHER[p][0]] + w * STRIDE[OTHER[p][1]])

    def near(p, a, b):
        return lax.rem(c[OTHER[p][0]] + a + SIDE, SIDE), lax.rem(c[OTHER[p][1]] + b + SIDE, SIDE)

    barrier = pltpu.get_barrier_semaphore()
    greet = [tuple(d if i == p else 0 for i in range(3)) for p in range(3) for d in range(1, SIDE)]
    for off in greet:
        y, z, x = (lax.rem(c[i] + off[i], SIDE) for i in range(3))
        pl.semaphore_signal(barrier, inc=1, device_id=(rep, y * 16 + z * 4 + x), device_id_type=MESH)
    pl.semaphore_signal(barrier, inc=1, device_id=(1 - rep, me), device_id_type=MESH)

    weights = [pltpu.make_async_copy(s.at[0], t, wsem.at[i])
               for i, (s, t) in enumerate(((wg_hbm, wg), (wu_hbm, wu), (wd_hbm, wd)))]
    mine = []
    for p in range(3):
        cols = pl.ds(0, COLS[p])
        mine.append(pltpu.make_async_copy(cc.at[p, c[p]], ids.at[p, c[p]], lsem.at[p]))
        mine.append(pltpu.make_async_copy(tok.at[:, pl.ds(OFF[p], COLS[p])], t_tok.at[p, c[p], :, cols], lsem.at[3 + p]))
        mine.append(pltpu.make_async_copy(cot.at[:, pl.ds(OFF[p], COLS[p])], t_cot.at[p, c[p], :, cols], lsem.at[6 + p]))
    for copy in mine:
        copy.start()
    pl.semaphore_wait(barrier, len(greet) + 1)

    outgoing = []
    for d in (2, 1, 3):
        for p in range(3):
            peer, v = axis_peer(p, d)
            outgoing.append(pltpu.make_async_remote_copy(
                cc.at[p, v], ids.at[p, c[p]], id_s.at[p, d - 1], id_r.at[p, d - 1], device_id=peer, device_id_type=MESH))
    for k, (src, dst) in enumerate(((tok, t_tok), (cot, t_cot))):
        for d in (1, 3):
            for p in range(3):
                peer, _ = axis_peer(p, d)
                outgoing.append(pltpu.make_async_remote_copy(
                    src.at[:, pl.ds(OFF[p], COLS[p])], dst.at[p, c[p], :, pl.ds(0, COLS[p])],
                    bc_s.at[k, p, d - 1], bc_r.at[k, p, d - 1], device_id=peer, device_id_type=MESH))
    for copy in outgoing:
        copy.start()
    for copy in weights:
        copy.start()

    def id_in(p, d):
        v = lax.rem(c[p] - d + SIDE, SIDE)
        return pltpu.make_async_remote_copy(
            cc.at[p, v], ids.at[p, v], id_s.at[p, d - 1], id_r.at[p, d - 1],
            device_id=axis_peer(p, d)[0], device_id_type=MESH)

    def bc_in(k, p, d):
        block = (t_tok, t_cot)[k].at[p, lax.rem(c[p] - d + SIDE, SIDE), :, pl.ds(0, COLS[p])]
        return pltpu.make_async_remote_copy(
            block, block, bc_s.at[k, p, d - 1], bc_r.at[k, p, d - 1], device_id=axis_peer(p, d)[0], device_id_type=MESH)

    def half(k, p, d, back):
        v = lax.rem(c[p] - (2 if back else d) + SIDE, SIDE)
        i = d // 2
        block = (t_tok, t_cot)[k].at[p, v, pl.ds(i * 64, 64), pl.ds(0, COLS[p])]
        return pltpu.make_async_remote_copy(
            block, block, hf_s.at[k, p, i], hf_r.at[k, p, i], device_id=axis_peer(p, d)[0], device_id_type=MESH)

    def forward(k):
        for d in (1, 3):
            for p in range(3):
                bc_in(k, p, d).wait_recv()
                copy = half(k, p, d, False)
                copy.start()
                outgoing.append(copy)

    for p in range(3):
        mine[3 * p].wait()
        for d in range(1, SIDE):
            id_in(p, d).wait_recv()

    FROM = (buf_a, buf_b, buf_a)
    SPREAD = (t_tok, t_cot)
    row16 = lax.broadcasted_iota(jnp.int32, (MAIN, TOK), 0).astype(F32)
    row8 = lax.broadcasted_iota(jnp.int32, (SIDE * EXTRA, TOK), 0)

    def main_mask(p, v, weigh):
        for uw in range(PLANE):
            code = ids[p, v, 0, uw:uw + 1, :]
            hit = jnp.broadcast_to(code, (MAIN, TOK)) == row16
            value = jnp.broadcast_to(ids[p, v, 1, uw:uw + 1, :], (MAIN, TOK)) if weigh else 1.0
            pm[uw * MAIN:(uw + 1) * MAIN, :] = jnp.where(hit, value, 0.0).astype(BF)

    def extra_mask(p, v, weigh):
        slot = (row8 % EXTRA + MAIN).astype(F32)
        blocks = []
        for uw in range(PLANE):
            code = jnp.broadcast_to(ids[p, v, 0, uw:uw + 1, :], row8.shape)
            value = jnp.broadcast_to(ids[p, v, 1, uw:uw + 1, :], row8.shape) if weigh else 1.0
            blocks.append(jnp.where((code == slot) & (row8 // EXTRA == v), value, 0.0))
        return jnp.concatenate(blocks, axis=0).astype(BF)

    def pick(k, p, d):
        n = COLS[p]
        v = lax.rem(c[p] - d + SIDE, SIDE)
        main_mask(p, v, k == 1)
        rows = pl.ds(pl.multiple_of(v * MAIN, MAIN), MAIN)
        got = jnp.dot(pm[...], SPREAD[k][p, v, :, 0:n], preferred_element_type=F32).astype(BF)
        FROM[k][p, :, rows, 0:n] = got.reshape(PLANE, MAIN, n)

    def pick_extra(k, p):
        n = COLS[p]
        got = jnp.zeros((PLANE * SIDE * EXTRA, n), F32)
        for v in range(SIDE):
            got += jnp.dot(extra_mask(p, v, k == 1), SPREAD[k][p, v, :, 0:n], preferred_element_type=F32)
        for uw in range(PLANE):
            FROM[k][p, uw, SIDE * MAIN:ROWS, 0:n] = got[uw * 8:uw * 8 + 8].astype(BF)

    def land(k, p, at):
        n = pl.ds(0, COLS[p])
        if k == 2 and p == 0:
            return r_last.at[at, :, n]
        return (x_hbm, c_hbm, r_hbm)[k].at[p, at, :, n]


    def hop(k, p, a, b, first):
        n = pl.ds(0, COLS[p])
        u, w = near(p, a, b)
        src = FROM[k].at[p, u * SIDE + w, :, n]
        if first:
            i = (a - 1) * 3 + b - 1
            dst, sem, to = y_hbm.at[k, p, i, :, n], y_r.at[k, p, i], plane_peer(p, u, c[OTHER[p][1]])
        else:
            dst, sem, to = land(k, p, own[p]), pl_r.at[k, p, a * SIDE + b], plane_peer(p, u, w)
        return pltpu.make_async_remote_copy(
            src, dst, pl_s.at[k, p, a * SIDE + b], sem, device_id=to, device_id_type=MESH)

    def relay(k, p, a, b):
        n = pl.ds(0, COLS[p])
        i = (a - 1) * 3 + b - 1
        u, _ = near(p, -a, 0)
        _, w = near(p, 0, b)
        block = y_hbm.at[k, p, i, :, n]
        to = plane_peer(p, c[OTHER[p][0]], w)
        pltpu.make_async_remote_copy(block, block, y_s.at[k, p, i], y_r.at[k, p, i],
                                     device_id=to, device_id_type=MESH).wait_recv()
        relay_copy(k, p, a, b, u, to).start()

    def relay_copy(k, p, a, b, u, to):
        n = pl.ds(0, COLS[p])
        i = (a - 1) * 3 + b - 1
        return pltpu.make_async_remote_copy(
            y_hbm.at[k, p, i, :, n], land(k, p, u * SIDE + c[OTHER[p][1]]),
            y_s.at[k, p, i], pl_r.at[k, p, a * SIDE + b], device_id=to, device_id_type=MESH)

    def relays(k, start, stop):
        def step(i, carry):
            for p in range(3):
                relay(k, p, i // 3 + 1, i % 3 + 1)
            return carry
        lax.fori_loop(start, stop, step, 0)

    def keep(k, p):
        n = pl.ds(0, COLS[p])
        return pltpu.make_async_copy(FROM[k].at[p, own[p], :, n], land(k, p, own[p]), ssem.at[k, p])

    def launch(k):
        for i in range(9):
            for p in range(3):
                hop(k, p, i // 3 + 1, i % 3 + 1, True).start()
        for a in (2, 1, 3):
            for p in range(3):
                hop(k, p, 0, a, False).start()
                hop(k, p, a, 0, False).start()
        for p in range(3):
            keep(k, p).start()

    def far(k, p):
        for d in (1, 3):
            half(k, p, d, True).wait_recv()

    forward(0)
    for p in range(3):
        mine[3 * p + 1].wait()
        for d in (0, 1, 3):
            pick(0, p, d)
    forward(1)
    for p in range(3):
        far(0, p)
        pick(0, p, 2)
        pick_extra(0, p)
    launch(0)
    for p in range(3):
        mine[3 * p + 2].wait()
        for d in (0, 1, 3):
            pick(1, p, d)
    for p in range(3):
        far(1, p)
        pick(1, p, 2)
        pick_extra(1, p)
    relays(0, 0, 9)
    launch(1)

    def arrived(k, p):
        keep(k, p).wait()

        def step(i, carry):
            u, w = near(p, -(i // SIDE), -(i % SIDE))
            block = land(k, p, u * SIDE + w)
            pltpu.make_async_remote_copy(block, block, pl_s.at[k, p, i], pl_r.at[k, p, i],
                                         device_id=plane_peer(p, u, w), device_id_type=MESH).wait_recv()
            return carry
        lax.fori_loop(1, PLANE, step, 0)

    def sent(k, p):
        def step(i, carry):
            n = pl.ds(0, COLS[p])
            u, w = near(p, i // SIDE, i % SIDE)
            block = FROM[k].at[p, u * SIDE + w, :, n]
            pltpu.make_async_remote_copy(block, block, pl_s.at[k, p, i], pl_r.at[k, p, i],
                                         device_id=plane_peer(p, u, w), device_id_type=MESH).wait_send()
            return carry
        lax.fori_loop(1, PLANE, step, 0)

    def relayed(k, p):
        def step(i, carry):
            a, b = i // 3 + 1, i % 3 + 1
            u, _ = near(p, -a, 0)
            _, w = near(p, 0, b)
            relay_copy(k, p, a, b, u, plane_peer(p, c[OTHER[p][0]], w)).wait_send()
            return carry
        lax.fori_loop(0, 9, step, 0)

    def stage_group(k, g, slot):
        src = (x_hbm, c_hbm)[k]
        for q in range(PLANE):
            z, x = q // SIDE, q % SIDE
            rows = pl.ds(q * MAIN, MAIN)
            pltpu.make_async_copy(
                src.at[0, q, pl.ds(pl.multiple_of(g * MAIN, MAIN), MAIN), :],
                stage.at[slot, rows, pl.ds(OFF[0], WIDE)], esem.at[slot]).start()
            pltpu.make_async_copy(
                src.at[1, x * SIDE + g, pl.ds(z * MAIN, MAIN), :],
                stage.at[slot, rows, pl.ds(OFF[1], WIDE)], esem.at[slot]).start()
            n = COLS[2]
            pltpu.make_async_copy(
                src.at[2, g * SIDE + z, pl.ds(x * MAIN, MAIN), pl.ds(0, n)],
                stage.at[slot, rows, pl.ds(OFF[2], n)], esem.at[slot]).start()

    def stage_wait(k, slot):
        pltpu.make_async_copy(stage.at[slot], stage.at[slot], esem.at[slot]).wait()

    def stage_extra(k):
        src = (x_hbm, c_hbm)[k]
        for p in range(3):
            for q in range(PLANE):
                pltpu.make_async_copy(
                    src.at[p, q, pl.ds(SIDE * MAIN, 8), pl.ds(0, COLS[p])],
                    ext.at[pl.ds(q * 8, 8), pl.ds(OFF[p], COLS[p])], esem.at[2]).start()
        pltpu.make_async_copy(ext, ext, esem.at[2]).wait()

    ra = lax.broadcasted_iota(jnp.int32, (128, 128), 0)
    rb = lax.broadcasted_iota(jnp.int32, (128, 128), 1)

    def plan_row(p, r):
        pos = (r // 32, (r // 8) % 4, (r // 2) % 4)
        return (pos[OTHER[p][0]] * 4 + pos[OTHER[p][1]]) * 8 + pos[p] * 2 + r % 2

    def to_canon(p):
        return (plan_row(p, ra) == rb).astype(F32).astype(BF)

    def from_canon(p):
        return (plan_row(p, rb) == ra).astype(F32).astype(BF)

    def extra_into_stage(k, slot):
        stage_extra(k)
        for p in range(3):
            cols = slice(OFF[p], OFF[p] + COLS[p])
            block = ext[:, cols]
            if p < 2:
                block = jnp.dot(to_canon(p), block, preferred_element_type=F32).astype(BF)
            stage[slot, 0:128, cols] = block

    def expert(slot, m, row0):
        def tile(i, carry):
            cols = pl.ds(pl.multiple_of(i * 256, 256), 256)
            gate = jnp.dot(stage[slot, 0:m, 0:D], wg[:, cols], preferred_element_type=F32)
            up = jnp.dot(stage[slot, 0:m, 0:D], wu[:, cols], preferred_element_type=F32)
            value = gate / (1.0 + jnp.exp(-gate)) * up
            act[pl.ds(row0, m), cols] = value
            hid[0:m, cols] = (scale[0:1, cols] * value).astype(BF)
            return carry
        lax.fori_loop(0, FF // 256, tile, 0)

    def down(m, p):
        return jnp.dot(hid[0:m, :], wd[:, OFF[p]:OFF[p] + COLS[p]], preferred_element_type=F32).astype(BF)

    for p in range(3):
        arrived(0, p)
    for p in range(3):
        sent(0, p)
    for copy in weights:
        copy.wait()
    stage_group(0, c[0], 0)
    extra_into_stage(0, 1)
    expert(1, 128, 1024)
    for p in range(3):
        out = down(128, p)
        if p < 2:
            out = jnp.dot(from_canon(p), out, preferred_element_type=F32).astype(BF)
        for q in range(PLANE):
            buf_a[p, q, SIDE * MAIN:ROWS, 0:COLS[p]] = out[q * 8:q * 8 + 8]

    def token_group(i, carry):
        slot = i % 2
        g = lax.rem(c[0] + i + SIDE, SIDE)
        stage_wait(0, slot)

        @pl.when(i < SIDE - 1)
        def _():
            stage_group(0, lax.rem(c[0] + i + 1 + SIDE, SIDE), 1 - slot)

        expert(slot, 256, pl.multiple_of(g * 256, 256))
        out = down(256, 2)
        buf_a[2, pl.ds(g * SIDE, SIDE), 0:SIDE * MAIN, 0:COLS[2]] = out.reshape(SIDE, SIDE * MAIN, COLS[2])
        out = down(256, 1)
        for z in range(SIDE):
            for x in range(SIDE):
                r = (z * SIDE + x) * MAIN
                buf_a[1, x * SIDE + g, z * MAIN:(z + 1) * MAIN, :] = out[r:r + MAIN]
        @pl.when(i == 0)
        def _():
            for a in (2, 1, 3):
                hop(2, 1, a, 0, False).start()
                hop(2, 2, 0, a, False).start()

        @pl.when(i > 0)
        def _():
            for a in (1, 2, 3):
                hop(2, 1, a, i, True).start()
                hop(2, 2, i, a, True).start()
            hop(2, 1, 0, i, False).start()
            hop(2, 2, i, 0, False).start()

        out = down(256, 0)
        buf_a[0, :, pl.ds(pl.multiple_of(g * MAIN, MAIN), MAIN), :] = out.reshape(PLANE, MAIN, COLS[0])
        relays(1, 2 * i, 2 * i + 2)
        return carry

    lax.fori_loop(0, SIDE, token_group, 0)
    for i in range(9):
        hop(2, 0, i // 3 + 1, i % 3 + 1, True).start()
    for a in (2, 1, 3):
        hop(2, 0, 0, a, False).start()
        hop(2, 0, a, 0, False).start()
    for p in range(3):
        keep(2, p).start()
    relays(1, 8, 9)

    def relay_returns(i, carry):
        for a in (1, 2, 3):
            relay(2, 1, a, i)
            relay(2, 2, i, a)
        return carry

    lax.fori_loop(1, SIDE, relay_returns, 0)

    def relay_last(i, carry):
        relay(2, 0, i // 3 + 1, i % 3 + 1)
        return carry

    lax.fori_loop(0, 9, relay_last, 0)

    for p in range(3):
        arrived(1, p)

    def gradient(slot, m, row0):
        def tile(i, carry):
            cols = pl.ds(pl.multiple_of(i * 256, 256), 256)
            back = lax.dot_general(stage[slot, 0:m, 0:D], wd[cols, :], (((1,), (1,)), ((), ())),
                                   preferred_element_type=F32)
            acc[0:1, cols] += jnp.sum(act[pl.ds(row0, m), cols] * back, axis=0, keepdims=True)
            return carry
        lax.fori_loop(0, FF // 256, tile, 0)

    acc[...] = jnp.zeros_like(acc)
    stage_group(1, c[0], 0)
    extra_into_stage(1, 1)
    gradient(1, 128, 1024)

    def cot_group(i, carry):
        slot = i % 2
        g = lax.rem(c[0] + i + SIDE, SIDE)
        stage_wait(1, slot)

        @pl.when(i < SIDE - 1)
        def _():
            stage_group(1, lax.rem(c[0] + i + 1 + SIDE, SIDE), 1 - slot)

        gradient(slot, 256, pl.multiple_of(g * 256, 256))
        return carry

    lax.fori_loop(0, SIDE, cot_group, 0)
    gsend[...] = acc[...]
    pair = pltpu.make_async_remote_copy(gsend, grecv, rep_s, rep_r, device_id=(1 - rep, me), device_id_type=MESH)
    pair.start()

    for p in range(3):
        sent(1, p)
    for copy in outgoing:
        copy.wait_send()
    red_out = []
    for p in (2, 1, 0):
        n = COLS[p]
        arrived(2, p)
        if p == 0:
            block = r_last
            left = jnp.concatenate([r_last[q, SIDE * MAIN:ROWS, :].astype(F32) for q in range(PLANE)], axis=0)
            ext[:, OFF[p]:OFF[p] + n] = left.astype(BF)
        else:
            block = buf_b.at[p]
            whole = pltpu.make_async_copy(r_hbm.at[p, :, :, pl.ds(0, n)], buf_b.at[p, :, :, pl.ds(0, n)], ssem.at[1, p])
            whole.start()
            for q in range(PLANE):
                pltpu.make_async_copy(
                    r_hbm.at[p, q, pl.ds(SIDE * MAIN, 8), pl.ds(0, n)],
                    ext.at[pl.ds(q * 8, 8), pl.ds(OFF[p], n)], esem.at[2]).start()
            e = ext.at[:, pl.ds(OFF[p], n)]
            pltpu.make_async_copy(e, e, esem.at[2]).wait()
            whole.wait()
        for d in (2, 1, 3, 0):
            peer, v = axis_peer(p, d)
            main_mask(p, v, True)
            rows = block[:, pl.ds(pl.multiple_of(v * MAIN, MAIN), MAIN), 0:n].reshape(PLANE * MAIN, n)
            total = lax.dot_general(pm[...], rows, (((0,), (0,)), ((), ())), preferred_element_type=F32)
            total += lax.dot_general(extra_mask(p, v, True), ext[:, OFF[p]:OFF[p] + n], (((0,), (0,)), ((), ())),
                                     preferred_element_type=F32)
            t_tok[p, d, :, 0:n] = total.astype(BF)
            src, dst = t_tok.at[p, d, :, pl.ds(0, n)], part.at[d, :, pl.ds(OFF[p], n)]
            if d == 0:
                copy = pltpu.make_async_copy(src, dst, lsem.at[p])
            else:
                copy = pltpu.make_async_remote_copy(
                    src, dst, red_s.at[p, d - 1], red_r.at[p, d - 1], device_id=peer, device_id_type=MESH)
            copy.start()
            red_out.append(copy)
    pair.wait()
    grad[...] = acc[0:1, :] + grecv[0:1, :]
    for p in range(3):
        sent(2, p)
        for k in range(3):
            relayed(k, p)
    for copy in red_out:
        copy.wait()


def shards(tokens, expert_ids, route_weights, cotangent, w_gate, w_up, w_down, ia3_scale):
    owners = 64
    ids_t = expert_ids.T
    weights_t = route_weights.T.astype(F32)
    hit = ids_t[:, None, :] == jnp.arange(owners, dtype=jnp.int32)[None, :, None]
    chosen = jnp.sum(hit.astype(F32), axis=0)
    weight = jnp.sum(jnp.where(hit, weights_t[:, None, :], 0.0), axis=0)
    earlier = jnp.arange(TOK)[:, None] < jnp.arange(TOK)[None, :]
    rank = jnp.dot(chosen.astype(BF), earlier.astype(BF), preferred_element_type=F32)
    code = jnp.where(chosen > 0, rank, 99.0)
    both = jnp.stack([code, weight]).reshape(2, 4, 4, 4, TOK)
    cc = jnp.stack([
        both.transpose(1, 0, 2, 3, 4).reshape(4, 2, 16, TOK),
        both.transpose(2, 0, 3, 1, 4).reshape(4, 2, 16, TOK),
        both.transpose(3, 0, 1, 2, 4).reshape(4, 2, 16, TOK),
    ])
    hbm = pl.BlockSpec(memory_space=pl.ANY)
    vmem = pl.BlockSpec(memory_space=pltpu.VMEM)
    land = jax.ShapeDtypeStruct((3, PLANE, ROWS, WIDE), BF)
    dma = pltpu.SemaphoreType.DMA
    out = pl.pallas_call(
        kernel,
        out_shape=[jax.ShapeDtypeStruct((SIDE, TOK, D), BF), jax.ShapeDtypeStruct((1, FF), F32), land, land, land,
                   jax.ShapeDtypeStruct((3, 3, 9, ROWS, WIDE), BF)],
        in_specs=[hbm] * 6 + [vmem],
        out_specs=[hbm, vmem, hbm, hbm, hbm, hbm],
        scratch_shapes=[
            pltpu.VMEM((3, SIDE, TOK, WIDE), BF),
            pltpu.VMEM((3, SIDE, TOK, WIDE), BF),
            pltpu.VMEM((3, PLANE, ROWS, WIDE), BF),
            pltpu.VMEM((3, PLANE, ROWS, WIDE), BF),
            pltpu.VMEM((PLANE, ROWS, WIDE), BF),
            pltpu.VMEM((3, SIDE, 2, PLANE, TOK), F32),
            pltpu.VMEM((D, FF), BF),
            pltpu.VMEM((D, FF), BF),
            pltpu.VMEM((FF, D), BF),
            pltpu.VMEM((1152, FF), F32),
            pltpu.VMEM((256, FF), BF),
            pltpu.VMEM((2, 256, D), BF),
            pltpu.VMEM((128, D), BF),
            pltpu.VMEM((256, TOK), BF),
            pltpu.VMEM((8, FF), F32),
            pltpu.VMEM((8, FF), F32),
            pltpu.VMEM((8, FF), F32),
            dma((3,)), dma((9,)), dma((3, 3)), dma((3,)),
            dma((3, 3)), dma((3, 3)), dma((2, 3, 3)), dma((2, 3, 3)), dma((2, 3, 2)), dma((2, 3, 2)),
            dma((3, 3, PLANE)), dma((3, 3, PLANE)), dma((3, 3, 9)), dma((3, 3, 9)), dma((3, 3)), dma((3, 3)), dma(()), dma(()),
        ],
        compiler_params=pltpu.CompilerParams(collective_id=0, has_side_effects=True, vmem_limit_bytes=67043328),
    )(tokens, cotangent, cc, w_gate, w_up, w_down, ia3_scale)
    return jnp.sum(out[0].astype(F32), axis=0).astype(BF), out[1]


def solution(mesh):
    rows = P(("rep", "exp"), None)
    weights = P("exp", None, None)
    return jax.shard_map(
        shards, mesh=mesh, in_specs=(rows, rows, rows, rows, weights, weights, weights, P("exp", None)),
        out_specs=(rows, P("exp", None)), check_vma=False)
```

```python
import jax
import jax.numpy as jnp
from jax import lax
from jax.experimental import pallas as pl
from jax.experimental.pallas import tpu as pltpu
from jax.sharding import PartitionSpec as P

MESH = pl.DeviceIdType.MESH
BF, F32 = jnp.bfloat16, jnp.float32
TOK, D, FF = 128, 4096, 768
SIDE, PLANE = 4, 16
MAIN, EXTRA, ROWS = 16, 2, 72
WIDE = 1408
COLS = ((1408, 1408, 1280), (1408, 1280, 1408), (1280, 1408, 1408))
OFF = tuple((0, n[0], n[0] + n[1]) for n in COLS)
STRIDE = (16, 4, 1)
OTHER = ((1, 2), (2, 0), (0, 1))


def kernel(tok, cot, cc, wg_hbm, wu_hbm, wd_hbm, scale, part, grad, x_hbm, c_hbm, r_hbm, y_hbm,
           t_tok, t_cot, buf_a, buf_b, r_last, ids, wg, wu, wd, act, hid, stage, ext, side, pm, acc, gsend, grecv,
           wsem, lsem, ssem, esem, id_s, id_r, bc_s, bc_r, hf_s, hf_r, pl_s, pl_r, y_s, y_r, sd_s, sd_r, red_s, red_r, rep_s, rep_r):
    rep = lax.axis_index("rep")
    me = lax.axis_index("exp")
    c = (me // 16, (me // 4) % 4, me % 4)
    own = [c[OTHER[p][0]] * SIDE + c[OTHER[p][1]] for p in range(3)]

    def axis_peer(p, d):
        v = lax.rem(c[p] + d, SIDE)
        return (rep, me + (v - c[p]) * STRIDE[p]), v

    def plane_peer(p, u, w):
        return (rep, c[p] * STRIDE[p] + u * STRIDE[OTHER[p][0]] + w * STRIDE[OTHER[p][1]])

    def near(p, a, b):
        return lax.rem(c[OTHER[p][0]] + a + SIDE, SIDE), lax.rem(c[OTHER[p][1]] + b + SIDE, SIDE)

    barrier = pltpu.get_barrier_semaphore()
    greet = [tuple(d if i == p else 0 for i in range(3)) for p in range(3) for d in range(1, SIDE)]
    for off in greet:
        y, z, x = (lax.rem(c[i] + off[i], SIDE) for i in range(3))
        pl.semaphore_signal(barrier, inc=1, device_id=(rep, y * 16 + z * 4 + x), device_id_type=MESH)
    pl.semaphore_signal(barrier, inc=1, device_id=(1 - rep, me), device_id_type=MESH)

    weights = [pltpu.make_async_copy(s.at[0], t, wsem.at[i])
               for i, (s, t) in enumerate(((wg_hbm, wg), (wu_hbm, wu), (wd_hbm, wd)))]
    mine = []
    for p in range(3):
        mine.append(pltpu.make_async_copy(cc.at[p, c[p]], ids.at[p, c[p]], lsem.at[p]))
        mine.append(pltpu.make_async_copy(tok.at[:, pl.ds(OFF[0][p], COLS[0][p])], t_tok.at[p, c[p], :, pl.ds(0, COLS[0][p])], lsem.at[3 + p]))
        mine.append(pltpu.make_async_copy(cot.at[:, pl.ds(OFF[1][p], COLS[1][p])], t_cot.at[p, c[p], :, pl.ds(0, COLS[1][p])], lsem.at[6 + p]))
    for copy in mine:
        copy.start()
    pl.semaphore_wait(barrier, len(greet) + 1)

    outgoing = []
    for d in (2, 1, 3):
        for p in range(3):
            peer, v = axis_peer(p, d)
            outgoing.append(pltpu.make_async_remote_copy(
                cc.at[p, v], ids.at[p, c[p]], id_s.at[p, d - 1], id_r.at[p, d - 1], device_id=peer, device_id_type=MESH))
    for k, (src, dst) in enumerate(((tok, t_tok), (cot, t_cot))):
        for d in (1, 3):
            for p in range(3):
                peer, _ = axis_peer(p, d)
                outgoing.append(pltpu.make_async_remote_copy(
                    src.at[:, pl.ds(OFF[k][p], COLS[k][p])], dst.at[p, c[p], :, pl.ds(0, COLS[k][p])],
                    bc_s.at[k, p, d - 1], bc_r.at[k, p, d - 1], device_id=peer, device_id_type=MESH))
    first = len(outgoing) - 6
    for copy in outgoing[:first]:
        copy.start()
    for copy in weights:
        copy.start()

    def id_in(p, d):
        v = lax.rem(c[p] - d + SIDE, SIDE)
        return pltpu.make_async_remote_copy(
            cc.at[p, v], ids.at[p, v], id_s.at[p, d - 1], id_r.at[p, d - 1],
            device_id=axis_peer(p, d)[0], device_id_type=MESH)

    def bc_in(k, p, d):
        block = (t_tok, t_cot)[k].at[p, lax.rem(c[p] - d + SIDE, SIDE), :, pl.ds(0, COLS[k][p])]
        return pltpu.make_async_remote_copy(
            block, block, bc_s.at[k, p, d - 1], bc_r.at[k, p, d - 1], device_id=axis_peer(p, d)[0], device_id_type=MESH)

    def half(k, p, d, back):
        v = lax.rem(c[p] - (2 if back else d) + SIDE, SIDE)
        i = d // 2
        block = (t_tok, t_cot)[k].at[p, v, pl.ds(i * 64, 64), pl.ds(0, COLS[k][p])]
        return pltpu.make_async_remote_copy(
            block, block, hf_s.at[k, p, i], hf_r.at[k, p, i], device_id=axis_peer(p, d)[0], device_id_type=MESH)

    def forward(k):
        for d in (1, 3):
            for p in range(3):
                bc_in(k, p, d).wait_recv()
                copy = half(k, p, d, False)
                copy.start()
                outgoing.append(copy)

    for p in range(3):
        mine[3 * p].wait()
        for d in range(1, SIDE):
            id_in(p, d).wait_recv()

    FROM = (buf_a, buf_b, buf_a)
    SPREAD = (t_tok, t_cot)
    row16 = lax.broadcasted_iota(jnp.int32, (MAIN, TOK), 0).astype(F32)
    row8 = lax.broadcasted_iota(jnp.int32, (SIDE * EXTRA, TOK), 0)

    def main_mask(p, v, weigh):
        for uw in range(PLANE):
            code = ids[p, v, 0, uw:uw + 1, :]
            hit = jnp.broadcast_to(code, (MAIN, TOK)) == row16
            value = jnp.broadcast_to(ids[p, v, 1, uw:uw + 1, :], (MAIN, TOK)) if weigh else 1.0
            pm[uw * MAIN:(uw + 1) * MAIN, :] = jnp.where(hit, value, 0.0).astype(BF)

    def extra_mask(p, v, weigh):
        slot = (row8 % EXTRA + MAIN).astype(F32)
        blocks = []
        for uw in range(PLANE):
            code = jnp.broadcast_to(ids[p, v, 0, uw:uw + 1, :], row8.shape)
            value = jnp.broadcast_to(ids[p, v, 1, uw:uw + 1, :], row8.shape) if weigh else 1.0
            blocks.append(jnp.where((code == slot) & (row8 // EXTRA == v), value, 0.0))
        return jnp.concatenate(blocks, axis=0).astype(BF)

    def pick(k, p, d):
        n = COLS[k][p]
        v = lax.rem(c[p] - d + SIDE, SIDE)
        main_mask(p, v, k == 1)
        rows = pl.ds(pl.multiple_of(v * MAIN, MAIN), MAIN)
        got = jnp.dot(pm[...], SPREAD[k][p, v, :, 0:n], preferred_element_type=F32).astype(BF)
        FROM[k][p, :, rows, 0:n] = got.reshape(PLANE, MAIN, n)

    def pick_extra(k, p):
        n = COLS[k][p]
        got = jnp.zeros((PLANE * SIDE * EXTRA, n), F32)
        for v in range(SIDE):
            got += jnp.dot(extra_mask(p, v, k == 1), SPREAD[k][p, v, :, 0:n], preferred_element_type=F32)
        for uw in range(PLANE):
            FROM[k][p, uw, SIDE * MAIN:ROWS, 0:n] = got[uw * 8:uw * 8 + 8].astype(BF)

    def land(k, p, at):
        n = pl.ds(0, COLS[k][p])
        if k == 2 and p == 0:
            return r_last.at[at, :, n]
        return (x_hbm, c_hbm, r_hbm)[k].at[p, at, :, n]


    def hop(k, p, a, b, first):
        n = pl.ds(0, COLS[k][p])
        u, w = near(p, a, b)
        src = FROM[k].at[p, u * SIDE + w, :, n]
        if first:
            i = (a - 1) * 3 + b - 1
            dst, sem, to = y_hbm.at[k, p, i, :, n], y_r.at[k, p, i], plane_peer(p, u, c[OTHER[p][1]])
        else:
            dst, sem, to = land(k, p, own[p]), pl_r.at[k, p, a * SIDE + b], plane_peer(p, u, w)
        return pltpu.make_async_remote_copy(
            src, dst, pl_s.at[k, p, a * SIDE + b], sem, device_id=to, device_id_type=MESH)

    def relay(k, p, a, b):
        n = pl.ds(0, COLS[k][p])
        i = (a - 1) * 3 + b - 1
        u, _ = near(p, -a, 0)
        _, w = near(p, 0, b)
        block = y_hbm.at[k, p, i, :, n]
        to = plane_peer(p, c[OTHER[p][0]], w)
        pltpu.make_async_remote_copy(block, block, y_s.at[k, p, i], y_r.at[k, p, i],
                                     device_id=to, device_id_type=MESH).wait_recv()
        relay_copy(k, p, a, b, u, to).start()

    def relay_copy(k, p, a, b, u, to):
        n = pl.ds(0, COLS[k][p])
        i = (a - 1) * 3 + b - 1
        return pltpu.make_async_remote_copy(
            y_hbm.at[k, p, i, :, n], land(k, p, u * SIDE + c[OTHER[p][1]]),
            y_s.at[k, p, i], pl_r.at[k, p, a * SIDE + b], device_id=to, device_id_type=MESH)

    def relays(k, start, stop):
        def step(i, carry):
            for p in range(3):
                relay(k, p, i // 3 + 1, i % 3 + 1)
            return carry
        lax.fori_loop(start, stop, step, 0)

    def keep(k, p):
        n = pl.ds(0, COLS[k][p])
        return pltpu.make_async_copy(FROM[k].at[p, own[p], :, n], land(k, p, own[p]), ssem.at[k, p])

    def launch_far(k, p):
        for i in range(9):
            hop(k, p, i // 3 + 1, i % 3 + 1, True).start()

    def launch_near(k):
        for a in (2, 1, 3):
            for p in range(3):
                hop(k, p, 0, a, False).start()
                hop(k, p, a, 0, False).start()
        for p in range(3):
            keep(k, p).start()

    def launch(k):
        for i in range(9):
            for p in range(3):
                hop(k, p, i // 3 + 1, i % 3 + 1, True).start()
        launch_near(k)

    def far(k, p):
        for d in (1, 3):
            half(k, p, d, True).wait_recv()

    cot_out = outgoing[first:]
    forward(0)
    for copy in cot_out:
        copy.start()
    for p in range(3):
        mine[3 * p + 1].wait()
        for d in (0, 1, 3):
            pick(0, p, d)
    for p in range(3):
        far(0, p)
        pick(0, p, 2)
        pick_extra(0, p)
        launch_far(0, p)
    launch_near(0)
    forward(1)
    for p in range(3):
        mine[3 * p + 2].wait()
        for d in (0, 1, 3):
            pick(1, p, d)
    relays(0, 0, 9)
    for p in range(3):
        far(1, p)
        pick(1, p, 2)
        pick_extra(1, p)
    launch(1)

    def arrived(k, p):
        keep(k, p).wait()

        def step(i, carry):
            u, w = near(p, -(i // SIDE), -(i % SIDE))
            block = land(k, p, u * SIDE + w)
            pltpu.make_async_remote_copy(block, block, pl_s.at[k, p, i], pl_r.at[k, p, i],
                                         device_id=plane_peer(p, u, w), device_id_type=MESH).wait_recv()
            return carry
        lax.fori_loop(1, PLANE, step, 0)

    def sent(k, p):
        def step(i, carry):
            n = pl.ds(0, COLS[k][p])
            u, w = near(p, i // SIDE, i % SIDE)
            block = FROM[k].at[p, u * SIDE + w, :, n]
            pltpu.make_async_remote_copy(block, block, pl_s.at[k, p, i], pl_r.at[k, p, i],
                                         device_id=plane_peer(p, u, w), device_id_type=MESH).wait_send()
            return carry
        lax.fori_loop(1, PLANE, step, 0)

    def relayed(k, p):
        def step(i, carry):
            a, b = i // 3 + 1, i % 3 + 1
            u, _ = near(p, -a, 0)
            _, w = near(p, 0, b)
            relay_copy(k, p, a, b, u, plane_peer(p, c[OTHER[p][0]], w)).wait_send()
            return carry
        lax.fori_loop(0, 9, step, 0)

    def stage_group(k, g, slot):
        src = (x_hbm, c_hbm)[k]
        for q in range(PLANE):
            z, x = q // SIDE, q % SIDE
            rows = pl.ds(q * MAIN, MAIN)
            pltpu.make_async_copy(
                src.at[0, q, pl.ds(pl.multiple_of(g * MAIN, MAIN), MAIN), pl.ds(0, COLS[k][0])],
                stage.at[slot, rows, pl.ds(OFF[k][0], COLS[k][0])], esem.at[slot]).start()
            pltpu.make_async_copy(
                src.at[1, x * SIDE + g, pl.ds(z * MAIN, MAIN), pl.ds(0, COLS[k][1])],
                stage.at[slot, rows, pl.ds(OFF[k][1], COLS[k][1])], esem.at[slot]).start()
            n = COLS[k][2]
            pltpu.make_async_copy(
                src.at[2, g * SIDE + z, pl.ds(x * MAIN, MAIN), pl.ds(0, n)],
                stage.at[slot, rows, pl.ds(OFF[k][2], n)], esem.at[slot]).start()

    def stage_wait(k, slot):
        pltpu.make_async_copy(stage.at[slot], stage.at[slot], esem.at[slot]).wait()

    def stage_extra(k):
        src = (x_hbm, c_hbm)[k]
        for p in range(3):
            for q in range(PLANE):
                pltpu.make_async_copy(
                    src.at[p, q, pl.ds(SIDE * MAIN, 8), pl.ds(0, COLS[k][p])],
                    ext.at[pl.ds(q * 8, 8), pl.ds(OFF[k][p], COLS[k][p])], esem.at[2]).start()
        pltpu.make_async_copy(ext, ext, esem.at[2]).wait()

    ra = lax.broadcasted_iota(jnp.int32, (128, 128), 0)
    rb = lax.broadcasted_iota(jnp.int32, (128, 128), 1)

    def plan_row(p, r):
        pos = (r // 32, (r // 8) % 4, (r // 2) % 4)
        return (pos[OTHER[p][0]] * 4 + pos[OTHER[p][1]]) * 8 + pos[p] * 2 + r % 2

    def to_canon(p):
        return (plan_row(p, ra) == rb).astype(F32).astype(BF)

    def from_canon(p):
        return (plan_row(p, rb) == ra).astype(F32).astype(BF)

    def extra_into_stage(k, slot):
        stage_extra(k)
        for p in range(3):
            cols = slice(OFF[k][p], OFF[k][p] + COLS[k][p])
            block = ext[:, cols]
            if p < 2:
                block = jnp.dot(to_canon(p), block, preferred_element_type=F32).astype(BF)
            stage[slot, 0:128, cols] = block

    def expert(slot, m, row0):
        def tile(i, carry):
            cols = pl.ds(pl.multiple_of(i * 256, 256), 256)
            gate = jnp.dot(stage[slot, 0:m, 0:D], wg[:, cols], preferred_element_type=F32)
            up = jnp.dot(stage[slot, 0:m, 0:D], wu[:, cols], preferred_element_type=F32)
            value = gate / (1.0 + jnp.exp(-gate)) * up
            act[pl.ds(row0, m), cols] = value
            hid[0:m, cols] = (scale[0:1, cols] * value).astype(BF)
            return carry
        lax.fori_loop(0, FF // 256, tile, 0)

    def down(m, p):
        return jnp.dot(hid[0:m, :], wd[:, OFF[2][p]:OFF[2][p] + COLS[2][p]], preferred_element_type=F32).astype(BF)

    for p in range(3):
        arrived(0, p)
    for p in range(3):
        sent(0, p)
    for copy in weights:
        copy.wait()
    stage_group(0, c[0], 0)
    extra_into_stage(0, 1)
    expert(1, 128, 1024)
    for p in range(3):
        out = down(128, p)
        if p < 2:
            out = jnp.dot(from_canon(p), out, preferred_element_type=F32).astype(BF)
        for q in range(PLANE):
            buf_a[p, q, SIDE * MAIN:ROWS, 0:COLS[2][p]] = out[q * 8:q * 8 + 8]

    def token_group(i, carry):
        slot = i % 2
        g = lax.rem(c[0] + i + SIDE, SIDE)
        stage_wait(0, slot)

        @pl.when(i < SIDE - 1)
        def _():
            stage_group(0, lax.rem(c[0] + i + 1 + SIDE, SIDE), 1 - slot)

        expert(slot, 256, pl.multiple_of(g * 256, 256))
        out = down(256, 2)
        buf_a[2, pl.ds(g * SIDE, SIDE), 0:SIDE * MAIN, 0:COLS[2][2]] = out.reshape(SIDE, SIDE * MAIN, COLS[2][2])
        out = down(256, 1)
        for z in range(SIDE):
            for x in range(SIDE):
                r = (z * SIDE + x) * MAIN
                buf_a[1, x * SIDE + g, z * MAIN:(z + 1) * MAIN, :] = out[r:r + MAIN]
        out = down(256, 0)
        buf_a[0, :, pl.ds(pl.multiple_of(g * MAIN, MAIN), MAIN), 0:COLS[2][0]] = out.reshape(PLANE, MAIN, COLS[2][0])
        relays(1, 2 * i, 2 * i + 2)
        return carry

    lax.fori_loop(0, SIDE, token_group, 0)
    launch(2)
    relays(1, 8, 9)
    relays(2, 0, 9)

    for p in range(3):
        arrived(1, p)

    def gradient(slot, m, row0):
        def tile(i, carry):
            cols = pl.ds(pl.multiple_of(i * 256, 256), 256)
            back = lax.dot_general(stage[slot, 0:m, 0:D], wd[cols, :], (((1,), (1,)), ((), ())),
                                   preferred_element_type=F32)
            acc[0:1, cols] += jnp.sum(act[pl.ds(row0, m), cols] * back, axis=0, keepdims=True)
            return carry
        lax.fori_loop(0, FF // 256, tile, 0)

    acc[...] = jnp.zeros_like(acc)
    stage_group(1, c[0], 0)
    extra_into_stage(1, 1)
    gradient(1, 128, 1024)

    def cot_group(i, carry):
        slot = i % 2
        g = lax.rem(c[0] + i + SIDE, SIDE)
        stage_wait(1, slot)

        @pl.when(i < SIDE - 1)
        def _():
            stage_group(1, lax.rem(c[0] + i + 1 + SIDE, SIDE), 1 - slot)

        gradient(slot, 256, pl.multiple_of(g * 256, 256))
        return carry

    lax.fori_loop(0, SIDE, cot_group, 0)
    gsend[...] = acc[...]
    pair = pltpu.make_async_remote_copy(gsend, grecv, rep_s, rep_r, device_id=(1 - rep, me), device_id_type=MESH)
    pair.start()

    for p in range(3):
        sent(1, p)
    for copy in outgoing:
        copy.wait_send()
    def fetch(p):
        n = COLS[2][p]
        whole = pltpu.make_async_copy(r_hbm.at[p, :, :, pl.ds(0, n)], buf_b.at[p, :, :, pl.ds(0, n)], ssem.at[1, p])
        whole.start()
        for q in range(PLANE):
            pltpu.make_async_copy(
                r_hbm.at[p, q, pl.ds(SIDE * MAIN, 8), pl.ds(0, n)],
                ext.at[pl.ds(q * 8, 8), pl.ds(OFF[2][p], n)], esem.at[p - 1]).start()
        return whole

    def weighted(p, d):
        n = COLS[2][p]
        v = lax.rem(c[p] + d, SIDE)
        block = r_last if p == 0 else buf_b.at[p]
        main_mask(p, v, True)
        rows = block[:, pl.ds(pl.multiple_of(v * MAIN, MAIN), MAIN), 0:n].reshape(PLANE * MAIN, n)
        total = lax.dot_general(pm[...], rows, (((0,), (0,)), ((), ())), preferred_element_type=F32)
        return total + lax.dot_general(extra_mask(p, v, True), ext[:, OFF[2][p]:OFF[2][p] + n], (((0,), (0,)), ((), ())),
                                       preferred_element_type=F32)

    def side_sum(p, i):
        n = pl.ds(0, COLS[2][p])
        return pltpu.make_async_remote_copy(
            t_tok.at[p, 2, pl.ds(i * 64, 64), n], side.at[p, i, :, n], sd_s.at[p, i], sd_r.at[p, i],
            device_id=axis_peer(p, 2 * i + 1)[0], device_id_type=MESH)

    def last_sum(p, i):
        n = COLS[2][p]
        d = 2 * i + 1
        return pltpu.make_async_remote_copy(
            t_tok.at[p, d, :, pl.ds(0, n)], part.at[1 + i, :, pl.ds(OFF[2][p], n)], red_s.at[p, i], red_r.at[p, i],
            device_id=axis_peer(p, d)[0], device_id_type=MESH)

    arrived(2, 2)
    loads = {2: fetch(2)}
    arrived(2, 1)
    loads[1] = fetch(1)
    arrived(2, 0)
    left = jnp.concatenate([r_last[q, SIDE * MAIN:ROWS, 0:COLS[2][0]].astype(F32) for q in range(PLANE)], axis=0)
    ext[:, 0:COLS[2][0]] = left.astype(BF)
    for p in (0, 2, 1):
        if p:
            e = ext.at[:, pl.ds(OFF[2][p], COLS[2][p])]
            pltpu.make_async_copy(e, e, esem.at[p - 1]).wait()
            loads[p].wait()
        t_tok[p, 2, :, 0:COLS[2][p]] = weighted(p, 2).astype(BF)
        for i in range(2):
            side_sum(p, i).start()
    mine = []
    for p in (0, 2, 1):
        n = COLS[2][p]
        for i in range(2):
            total = weighted(p, 2 * i + 1)
            side_sum(p, i).wait_recv()
            added = total[i * 64:i * 64 + 64] + side[p, i, :, 0:n].astype(F32)
            t_tok[p, 2 * i + 1, i * 64:i * 64 + 64, 0:n] = added.astype(BF)
            t_tok[p, 2 * i + 1, 64 - i * 64:128 - i * 64, 0:n] = total[64 - i * 64:128 - i * 64].astype(BF)
            last_sum(p, i).start()
    for p in (0, 2, 1):
        n = COLS[2][p]
        t_tok[p, 0, :, 0:n] = weighted(p, 0).astype(BF)
        copy = pltpu.make_async_copy(t_tok.at[p, 0, :, pl.ds(0, n)], part.at[0, :, pl.ds(OFF[2][p], n)], lsem.at[p])
        copy.start()
        mine.append(copy)
    pair.wait()
    grad[...] = acc[0:1, :] + grecv[0:1, :]
    for p in range(3):
        sent(2, p)
        for k in range(3):
            relayed(k, p)
    for copy in mine:
        copy.wait()
    for p in range(3):
        for i in range(2):
            side_sum(p, i).wait_send()
            last_sum(p, i).wait()


def shards(tokens, expert_ids, route_weights, cotangent, w_gate, w_up, w_down, ia3_scale):
    owners = 64
    ids_t = expert_ids.T
    weights_t = route_weights.T.astype(F32)
    hit = ids_t[:, None, :] == jnp.arange(owners, dtype=jnp.int32)[None, :, None]
    chosen = jnp.sum(hit.astype(F32), axis=0)
    weight = jnp.sum(jnp.where(hit, weights_t[:, None, :], 0.0), axis=0)
    earlier = jnp.arange(TOK)[:, None] < jnp.arange(TOK)[None, :]
    rank = jnp.dot(chosen.astype(BF), earlier.astype(BF), preferred_element_type=F32)
    code = jnp.where(chosen > 0, rank, 99.0)
    both = jnp.stack([code, weight]).reshape(2, 4, 4, 4, TOK)
    cc = jnp.stack([
        both.transpose(1, 0, 2, 3, 4).reshape(4, 2, 16, TOK),
        both.transpose(2, 0, 3, 1, 4).reshape(4, 2, 16, TOK),
        both.transpose(3, 0, 1, 2, 4).reshape(4, 2, 16, TOK),
    ])
    hbm = pl.BlockSpec(memory_space=pl.ANY)
    vmem = pl.BlockSpec(memory_space=pltpu.VMEM)
    land = jax.ShapeDtypeStruct((3, PLANE, ROWS, WIDE), BF)
    dma = pltpu.SemaphoreType.DMA
    out = pl.pallas_call(
        kernel,
        out_shape=[jax.ShapeDtypeStruct((3, TOK, D), BF), jax.ShapeDtypeStruct((1, FF), F32), land, land, land,
                   jax.ShapeDtypeStruct((3, 3, 9, ROWS, WIDE), BF)],
        in_specs=[hbm] * 6 + [vmem],
        out_specs=[hbm, vmem, hbm, hbm, hbm, hbm],
        scratch_shapes=[
            pltpu.VMEM((3, SIDE, TOK, WIDE), BF),
            pltpu.VMEM((3, SIDE, TOK, WIDE), BF),
            pltpu.VMEM((3, PLANE, ROWS, WIDE), BF),
            pltpu.VMEM((3, PLANE, ROWS, WIDE), BF),
            pltpu.VMEM((PLANE, ROWS, WIDE), BF),
            pltpu.VMEM((3, SIDE, 2, PLANE, TOK), F32),
            pltpu.VMEM((D, FF), BF),
            pltpu.VMEM((D, FF), BF),
            pltpu.VMEM((FF, D), BF),
            pltpu.VMEM((1152, FF), F32),
            pltpu.VMEM((256, FF), BF),
            pltpu.VMEM((2, 256, D), BF),
            pltpu.VMEM((128, D), BF),
            pltpu.VMEM((3, 2, 64, WIDE), BF),
            pltpu.VMEM((256, TOK), BF),
            pltpu.VMEM((8, FF), F32),
            pltpu.VMEM((8, FF), F32),
            pltpu.VMEM((8, FF), F32),
            dma((3,)), dma((9,)), dma((3, 3)), dma((3,)),
            dma((3, 3)), dma((3, 3)), dma((2, 3, 3)), dma((2, 3, 3)), dma((2, 3, 2)), dma((2, 3, 2)),
            dma((3, 3, PLANE)), dma((3, 3, PLANE)), dma((3, 3, 9)), dma((3, 3, 9)), dma((3, 2)), dma((3, 2)), dma((3, 2)), dma((3, 2)), dma(()), dma(()),
        ],
        compiler_params=pltpu.CompilerParams(collective_id=0, has_side_effects=True, vmem_limit_bytes=67043328),
    )(tokens, cotangent, cc, w_gate, w_up, w_down, ia3_scale)
    return jnp.sum(out[0].astype(F32), axis=0).astype(BF), out[1]


def solution(mesh):
    rows = P(("rep", "exp"), None)
    weights = P("exp", None, None)
    return jax.shard_map(
        shards, mesh=mesh, in_specs=(rows, rows, rows, rows, weights, weights, weights, P("exp", None)),
        out_specs=(rows, P("exp", None)), check_vma=False)
```

```python
import jax
import jax.numpy as jnp
from jax import lax
from jax.experimental import pallas as pl
from jax.experimental.pallas import tpu as pltpu
from jax.sharding import PartitionSpec as P

MESH = pl.DeviceIdType.MESH
BF, F32 = jnp.bfloat16, jnp.float32
TOK, D, FF = 128, 4096, 768
SIDE, PLANE = 4, 16
MAIN, EXTRA, ROWS = 16, 2, 72
WIDE = 1408
COLS = ((1408, 1408, 1280), (1408, 1280, 1408), (1280, 1408, 1408))
OFF = tuple((0, n[0], n[0] + n[1]) for n in COLS)
STRIDE = (16, 4, 1)
OTHER = ((1, 2), (2, 0), (0, 1))


def kernel(tok, cot, cc, wg_hbm, wu_hbm, wd_hbm, scale, part, grad, x_hbm, c_hbm, r_hbm, y_hbm,
           t_tok, t_cot, buf_a, buf_b, r_last, ids, wg, wu, wd, act, hid, stage, ext, side, mix, pm, acc, gsend, grecv,
           wsem, lsem, ssem, esem, id_s, id_r, bc_s, bc_r, hf_s, hf_r, pl_s, pl_r, y_s, y_r, sd_s, sd_r, red_s, red_r, rep_s, rep_r):
    rep = lax.axis_index("rep")
    me = lax.axis_index("exp")
    c = (me // 16, (me // 4) % 4, me % 4)
    own = [c[OTHER[p][0]] * SIDE + c[OTHER[p][1]] for p in range(3)]

    def axis_peer(p, d):
        v = lax.rem(c[p] + d, SIDE)
        return (rep, me + (v - c[p]) * STRIDE[p]), v

    def plane_peer(p, u, w):
        return (rep, c[p] * STRIDE[p] + u * STRIDE[OTHER[p][0]] + w * STRIDE[OTHER[p][1]])

    def near(p, a, b):
        return lax.rem(c[OTHER[p][0]] + a + SIDE, SIDE), lax.rem(c[OTHER[p][1]] + b + SIDE, SIDE)

    barrier = pltpu.get_barrier_semaphore()
    greet = [tuple(d if i == p else 0 for i in range(3)) for p in range(3) for d in range(1, SIDE)]
    for off in greet:
        y, z, x = (lax.rem(c[i] + off[i], SIDE) for i in range(3))
        pl.semaphore_signal(barrier, inc=1, device_id=(rep, y * 16 + z * 4 + x), device_id_type=MESH)
    pl.semaphore_signal(barrier, inc=1, device_id=(1 - rep, me), device_id_type=MESH)

    weights = [pltpu.make_async_copy(s.at[0], t, wsem.at[i])
               for i, (s, t) in enumerate(((wg_hbm, wg), (wu_hbm, wu), (wd_hbm, wd)))]
    mine = []
    for p in range(3):
        mine.append(pltpu.make_async_copy(cc.at[p, c[p]], ids.at[p, c[p]], lsem.at[p]))
        mine.append(pltpu.make_async_copy(tok.at[:, pl.ds(OFF[0][p], COLS[0][p])], t_tok.at[p, c[p], :, pl.ds(0, COLS[0][p])], lsem.at[3 + p]))
        mine.append(pltpu.make_async_copy(cot.at[:, pl.ds(OFF[1][p], COLS[1][p])], t_cot.at[p, c[p], :, pl.ds(0, COLS[1][p])], lsem.at[6 + p]))
    for copy in mine:
        copy.start()
    pl.semaphore_wait(barrier, len(greet) + 1)

    outgoing = []
    for d in (2, 1, 3):
        for p in range(3):
            peer, v = axis_peer(p, d)
            outgoing.append(pltpu.make_async_remote_copy(
                cc.at[p, v], ids.at[p, c[p]], id_s.at[p, d - 1], id_r.at[p, d - 1], device_id=peer, device_id_type=MESH))
    for k, (src, dst) in enumerate(((tok, t_tok), (cot, t_cot))):
        for d in (1, 3):
            for p in range(3):
                peer, _ = axis_peer(p, d)
                outgoing.append(pltpu.make_async_remote_copy(
                    src.at[:, pl.ds(OFF[k][p], COLS[k][p])], dst.at[p, c[p], :, pl.ds(0, COLS[k][p])],
                    bc_s.at[k, p, d - 1], bc_r.at[k, p, d - 1], device_id=peer, device_id_type=MESH))
    first = len(outgoing) - 6
    for copy in outgoing[:first]:
        copy.start()
    for copy in weights:
        copy.start()

    def id_in(p, d):
        v = lax.rem(c[p] - d + SIDE, SIDE)
        return pltpu.make_async_remote_copy(
            cc.at[p, v], ids.at[p, v], id_s.at[p, d - 1], id_r.at[p, d - 1],
            device_id=axis_peer(p, d)[0], device_id_type=MESH)

    def bc_in(k, p, d):
        block = (t_tok, t_cot)[k].at[p, lax.rem(c[p] - d + SIDE, SIDE), :, pl.ds(0, COLS[k][p])]
        return pltpu.make_async_remote_copy(
            block, block, bc_s.at[k, p, d - 1], bc_r.at[k, p, d - 1], device_id=axis_peer(p, d)[0], device_id_type=MESH)

    def half(k, p, d, back):
        v = lax.rem(c[p] - (2 if back else d) + SIDE, SIDE)
        i = d // 2
        block = (t_tok, t_cot)[k].at[p, v, pl.ds(i * 64, 64), pl.ds(0, COLS[k][p])]
        return pltpu.make_async_remote_copy(
            block, block, hf_s.at[k, p, i], hf_r.at[k, p, i], device_id=axis_peer(p, d)[0], device_id_type=MESH)

    def forward(k):
        for d in (1, 3):
            for p in range(3):
                bc_in(k, p, d).wait_recv()
                copy = half(k, p, d, False)
                copy.start()
                outgoing.append(copy)

    for p in range(3):
        mine[3 * p].wait()
        for d in range(1, SIDE):
            id_in(p, d).wait_recv()

    FROM = (buf_a, buf_b, buf_a)
    SPREAD = (t_tok, t_cot)
    row16 = lax.broadcasted_iota(jnp.int32, (MAIN, TOK), 0).astype(F32)
    row8 = lax.broadcasted_iota(jnp.int32, (SIDE * EXTRA, TOK), 0)

    def main_mask(p, v, weigh):
        for uw in range(PLANE):
            code = ids[p, v, 0, uw:uw + 1, :]
            hit = jnp.broadcast_to(code, (MAIN, TOK)) == row16
            value = jnp.broadcast_to(ids[p, v, 1, uw:uw + 1, :], (MAIN, TOK)) if weigh else 1.0
            pm[uw * MAIN:(uw + 1) * MAIN, :] = jnp.where(hit, value, 0.0).astype(BF)

    def extra_mask(p, v, weigh):
        slot = (row8 % EXTRA + MAIN).astype(F32)
        blocks = []
        for uw in range(PLANE):
            code = jnp.broadcast_to(ids[p, v, 0, uw:uw + 1, :], row8.shape)
            value = jnp.broadcast_to(ids[p, v, 1, uw:uw + 1, :], row8.shape) if weigh else 1.0
            blocks.append(jnp.where((code == slot) & (row8 // EXTRA == v), value, 0.0))
        return jnp.concatenate(blocks, axis=0).astype(BF)

    def pick(k, p, d):
        n = COLS[k][p]
        v = lax.rem(c[p] - d + SIDE, SIDE)
        main_mask(p, v, k == 1)
        rows = pl.ds(pl.multiple_of(v * MAIN, MAIN), MAIN)
        got = jnp.dot(pm[...], SPREAD[k][p, v, :, 0:n], preferred_element_type=F32).astype(BF)
        FROM[k][p, :, rows, 0:n] = got.reshape(PLANE, MAIN, n)

    def pick_extra(k, p):
        n = COLS[k][p]
        got = jnp.zeros((PLANE * SIDE * EXTRA, n), F32)
        for v in range(SIDE):
            got += jnp.dot(extra_mask(p, v, k == 1), SPREAD[k][p, v, :, 0:n], preferred_element_type=F32)
        for uw in range(PLANE):
            FROM[k][p, uw, SIDE * MAIN:ROWS, 0:n] = got[uw * 8:uw * 8 + 8].astype(BF)

    def land(k, p, at):
        n = pl.ds(0, COLS[k][p])
        if k == 2 and p == 0:
            return r_last.at[at, :, n]
        return (x_hbm, c_hbm, r_hbm)[k].at[p, at, :, n]


    def hop(k, p, a, b, first):
        n = pl.ds(0, COLS[k][p])
        u, w = near(p, a, b)
        src = FROM[k].at[p, u * SIDE + w, :, n]
        if first:
            i = (a - 1) * 3 + b - 1
            dst, sem, to = y_hbm.at[k, p, i, :, n], y_r.at[k, p, i], plane_peer(p, u, c[OTHER[p][1]])
        else:
            dst, sem, to = land(k, p, own[p]), pl_r.at[k, p, a * SIDE + b], plane_peer(p, u, w)
        return pltpu.make_async_remote_copy(
            src, dst, pl_s.at[k, p, a * SIDE + b], sem, device_id=to, device_id_type=MESH)

    def relay(k, p, a, b):
        n = pl.ds(0, COLS[k][p])
        i = (a - 1) * 3 + b - 1
        u, _ = near(p, -a, 0)
        _, w = near(p, 0, b)
        block = y_hbm.at[k, p, i, :, n]
        to = plane_peer(p, c[OTHER[p][0]], w)
        pltpu.make_async_remote_copy(block, block, y_s.at[k, p, i], y_r.at[k, p, i],
                                     device_id=to, device_id_type=MESH).wait_recv()
        relay_copy(k, p, a, b, u, to).start()

    def relay_copy(k, p, a, b, u, to):
        n = pl.ds(0, COLS[k][p])
        i = (a - 1) * 3 + b - 1
        return pltpu.make_async_remote_copy(
            y_hbm.at[k, p, i, :, n], land(k, p, u * SIDE + c[OTHER[p][1]]),
            y_s.at[k, p, i], pl_r.at[k, p, a * SIDE + b], device_id=to, device_id_type=MESH)

    def relays(k, start, stop):
        def step(i, carry):
            for p in range(3):
                relay(k, p, i // 3 + 1, i % 3 + 1)
            return carry
        lax.fori_loop(start, stop, step, 0)

    def keep(k, p):
        n = pl.ds(0, COLS[k][p])
        return pltpu.make_async_copy(FROM[k].at[p, own[p], :, n], land(k, p, own[p]), ssem.at[k, p])

    def launch_far(k, p):
        for i in range(9):
            hop(k, p, i // 3 + 1, i % 3 + 1, True).start()

    def launch_near(k):
        for a in (2, 1, 3):
            for p in range(3):
                hop(k, p, 0, a, False).start()
                hop(k, p, a, 0, False).start()
        for p in range(3):
            keep(k, p).start()

    def launch(k):
        for i in range(9):
            for p in range(3):
                hop(k, p, i // 3 + 1, i % 3 + 1, True).start()
        launch_near(k)

    def far(k, p):
        for d in (1, 3):
            half(k, p, d, True).wait_recv()

    cot_out = outgoing[first:]
    for p in range(3):
        mine[3 * p + 1].wait()
        pick(0, p, 0)
    forward(0)
    for copy in cot_out:
        copy.start()
    for p in range(3):
        for d in (1, 3):
            pick(0, p, d)
    for p in range(3):
        far(0, p)
        pick(0, p, 2)
        pick_extra(0, p)
        launch_far(0, p)
    launch_near(0)
    forward(1)
    for p in range(3):
        mine[3 * p + 2].wait()
        for d in (0, 1, 3):
            pick(1, p, d)
    relays(0, 0, 9)
    for p in range(3):
        far(1, p)
        pick(1, p, 2)
        pick_extra(1, p)
    launch(1)

    def arrived(k, p):
        keep(k, p).wait()

        def step(i, carry):
            u, w = near(p, -(i // SIDE), -(i % SIDE))
            block = land(k, p, u * SIDE + w)
            pltpu.make_async_remote_copy(block, block, pl_s.at[k, p, i], pl_r.at[k, p, i],
                                         device_id=plane_peer(p, u, w), device_id_type=MESH).wait_recv()
            return carry
        lax.fori_loop(1, PLANE, step, 0)

    def sent(k, p):
        def step(i, carry):
            n = pl.ds(0, COLS[k][p])
            u, w = near(p, i // SIDE, i % SIDE)
            block = FROM[k].at[p, u * SIDE + w, :, n]
            pltpu.make_async_remote_copy(block, block, pl_s.at[k, p, i], pl_r.at[k, p, i],
                                         device_id=plane_peer(p, u, w), device_id_type=MESH).wait_send()
            return carry
        lax.fori_loop(1, PLANE, step, 0)

    def relayed(k, p):
        def step(i, carry):
            a, b = i // 3 + 1, i % 3 + 1
            u, _ = near(p, -a, 0)
            _, w = near(p, 0, b)
            relay_copy(k, p, a, b, u, plane_peer(p, c[OTHER[p][0]], w)).wait_send()
            return carry
        lax.fori_loop(0, 9, step, 0)

    def stage_group(k, g, slot):
        src = (x_hbm, c_hbm)[k]
        for q in range(PLANE):
            z, x = q // SIDE, q % SIDE
            rows = pl.ds(q * MAIN, MAIN)
            pltpu.make_async_copy(
                src.at[0, q, pl.ds(pl.multiple_of(g * MAIN, MAIN), MAIN), pl.ds(0, COLS[k][0])],
                stage.at[slot, rows, pl.ds(OFF[k][0], COLS[k][0])], esem.at[slot]).start()
            pltpu.make_async_copy(
                src.at[1, x * SIDE + g, pl.ds(z * MAIN, MAIN), pl.ds(0, COLS[k][1])],
                stage.at[slot, rows, pl.ds(OFF[k][1], COLS[k][1])], esem.at[slot]).start()
            n = COLS[k][2]
            pltpu.make_async_copy(
                src.at[2, g * SIDE + z, pl.ds(x * MAIN, MAIN), pl.ds(0, n)],
                stage.at[slot, rows, pl.ds(OFF[k][2], n)], esem.at[slot]).start()

    def stage_wait(k, slot):
        pltpu.make_async_copy(stage.at[slot], stage.at[slot], esem.at[slot]).wait()

    def stage_extra(k):
        src = (x_hbm, c_hbm)[k]
        for p in range(3):
            for q in range(PLANE):
                pltpu.make_async_copy(
                    src.at[p, q, pl.ds(SIDE * MAIN, 8), pl.ds(0, COLS[k][p])],
                    ext.at[pl.ds(q * 8, 8), pl.ds(OFF[k][p], COLS[k][p])], esem.at[2]).start()
        pltpu.make_async_copy(ext, ext, esem.at[2]).wait()

    ra = lax.broadcasted_iota(jnp.int32, (128, 128), 0)
    rb = lax.broadcasted_iota(jnp.int32, (128, 128), 1)

    def plan_row(p, r):
        pos = (r // 32, (r // 8) % 4, (r // 2) % 4)
        return (pos[OTHER[p][0]] * 4 + pos[OTHER[p][1]]) * 8 + pos[p] * 2 + r % 2

    def to_canon(p):
        return (plan_row(p, ra) == rb).astype(F32).astype(BF)

    def from_canon(p):
        return (plan_row(p, rb) == ra).astype(F32).astype(BF)

    def extra_into_stage(k, slot):
        stage_extra(k)
        for p in range(3):
            cols = slice(OFF[k][p], OFF[k][p] + COLS[k][p])
            block = ext[:, cols]
            if p < 2:
                block = jnp.dot(to_canon(p), block, preferred_element_type=F32).astype(BF)
            stage[slot, 0:128, cols] = block

    def expert(slot, m, row0):
        def tile(i, carry):
            cols = pl.ds(pl.multiple_of(i * 256, 256), 256)
            gate = jnp.dot(stage[slot, 0:m, 0:D], wg[:, cols], preferred_element_type=F32)
            up = jnp.dot(stage[slot, 0:m, 0:D], wu[:, cols], preferred_element_type=F32)
            value = gate / (1.0 + jnp.exp(-gate)) * up
            act[pl.ds(row0, m), cols] = value
            hid[0:m, cols] = (scale[0:1, cols] * value).astype(BF)
            return carry
        lax.fori_loop(0, FF // 256, tile, 0)

    def down(m, p):
        return jnp.dot(hid[0:m, :], wd[:, OFF[2][p]:OFF[2][p] + COLS[2][p]], preferred_element_type=F32).astype(BF)

    for p in range(3):
        arrived(0, p)
    for p in range(3):
        sent(0, p)
    for copy in weights:
        copy.wait()
    stage_group(0, c[0], 0)
    extra_into_stage(0, 1)
    expert(1, 128, 1024)
    for p in range(3):
        out = down(128, p)
        if p < 2:
            out = jnp.dot(from_canon(p), out, preferred_element_type=F32).astype(BF)
        for q in range(PLANE):
            buf_a[p, q, SIDE * MAIN:ROWS, 0:COLS[2][p]] = out[q * 8:q * 8 + 8]

    def token_group(i, carry):
        slot = i % 2
        g = lax.rem(c[0] + i + SIDE, SIDE)
        stage_wait(0, slot)

        @pl.when(i < SIDE - 1)
        def _():
            stage_group(0, lax.rem(c[0] + i + 1 + SIDE, SIDE), 1 - slot)

        expert(slot, 256, pl.multiple_of(g * 256, 256))
        out = down(256, 2)
        buf_a[2, pl.ds(g * SIDE, SIDE), 0:SIDE * MAIN, 0:COLS[2][2]] = out.reshape(SIDE, SIDE * MAIN, COLS[2][2])
        out = down(256, 1)
        for z in range(SIDE):
            for x in range(SIDE):
                r = (z * SIDE + x) * MAIN
                buf_a[1, x * SIDE + g, z * MAIN:(z + 1) * MAIN, :] = out[r:r + MAIN]
        out = down(256, 0)
        buf_a[0, :, pl.ds(pl.multiple_of(g * MAIN, MAIN), MAIN), 0:COLS[2][0]] = out.reshape(PLANE, MAIN, COLS[2][0])
        relays(1, 2 * i, 2 * i + 2)
        return carry

    lax.fori_loop(0, SIDE, token_group, 0)
    launch(2)
    relays(1, 8, 9)
    relays(2, 0, 9)

    for p in range(3):
        arrived(1, p)

    def gradient(slot, m, row0):
        def tile(i, carry):
            cols = pl.ds(pl.multiple_of(i * 256, 256), 256)
            back = lax.dot_general(stage[slot, 0:m, 0:D], wd[cols, :], (((1,), (1,)), ((), ())),
                                   preferred_element_type=F32)
            acc[0:1, cols] += jnp.sum(act[pl.ds(row0, m), cols] * back, axis=0, keepdims=True)
            return carry
        lax.fori_loop(0, FF // 256, tile, 0)

    acc[...] = jnp.zeros_like(acc)
    stage_group(1, c[0], 0)
    extra_into_stage(1, 1)
    gradient(1, 128, 1024)

    def cot_group(i, carry):
        slot = i % 2
        g = lax.rem(c[0] + i + SIDE, SIDE)
        stage_wait(1, slot)

        @pl.when(i < SIDE - 1)
        def _():
            stage_group(1, lax.rem(c[0] + i + 1 + SIDE, SIDE), 1 - slot)

        gradient(slot, 256, pl.multiple_of(g * 256, 256))
        return carry

    lax.fori_loop(0, SIDE, cot_group, 0)
    gsend[...] = acc[...]
    pair = pltpu.make_async_remote_copy(gsend, grecv, rep_s, rep_r, device_id=(1 - rep, me), device_id_type=MESH)
    pair.start()

    for p in range(3):
        sent(1, p)
    for copy in outgoing:
        copy.wait_send()
    def fetch(p):
        n = COLS[2][p]
        whole = pltpu.make_async_copy(r_hbm.at[p, :, :, pl.ds(0, n)], buf_b.at[p, :, :, pl.ds(0, n)], ssem.at[1, p])
        whole.start()
        for q in range(PLANE):
            pltpu.make_async_copy(
                r_hbm.at[p, q, pl.ds(SIDE * MAIN, 8), pl.ds(0, n)],
                ext.at[pl.ds(q * 8, 8), pl.ds(OFF[2][p], n)], esem.at[p - 1]).start()
        return whole

    def weighted(p, d):
        n = COLS[2][p]
        v = lax.rem(c[p] + d, SIDE)
        block = r_last if p == 0 else buf_b.at[p]
        rows = block[:, pl.ds(pl.multiple_of(v * MAIN, MAIN), MAIN), 0:n].reshape(PLANE * MAIN, n)
        total = jnp.dot(mix[p, d, :, 0:256], rows, preferred_element_type=F32)
        return total + jnp.dot(mix[p, d, :, 256:384], ext[:, OFF[2][p]:OFF[2][p] + n], preferred_element_type=F32)

    def side_sum(p, i):
        n = pl.ds(0, COLS[2][p])
        return pltpu.make_async_remote_copy(
            t_tok.at[p, 2, pl.ds(i * 64, 64), n], side.at[p, i, :, n], sd_s.at[p, i], sd_r.at[p, i],
            device_id=axis_peer(p, 2 * i + 1)[0], device_id_type=MESH)

    def last_sum(p, i):
        n = COLS[2][p]
        d = 2 * i + 1
        return pltpu.make_async_remote_copy(
            t_tok.at[p, d, :, pl.ds(0, n)], part.at[1 + i, :, pl.ds(OFF[2][p], n)], red_s.at[p, i], red_r.at[p, i],
            device_id=axis_peer(p, d)[0], device_id_type=MESH)

    for p in range(3):
        for d in range(SIDE):
            v = lax.rem(c[p] + d, SIDE)
            main_mask(p, v, True)
            mix[p, d, :, 0:256] = pm[...].astype(F32).T.astype(BF)
            mix[p, d, :, 256:384] = extra_mask(p, v, True).astype(F32).T.astype(BF)
    arrived(2, 2)
    loads = {2: fetch(2)}
    arrived(2, 1)
    loads[1] = fetch(1)
    arrived(2, 0)
    left = jnp.concatenate([r_last[q, SIDE * MAIN:ROWS, 0:COLS[2][0]].astype(F32) for q in range(PLANE)], axis=0)
    ext[:, 0:COLS[2][0]] = left.astype(BF)
    for p in (0, 2, 1):
        if p:
            e = ext.at[:, pl.ds(OFF[2][p], COLS[2][p])]
            pltpu.make_async_copy(e, e, esem.at[p - 1]).wait()
            loads[p].wait()
        t_tok[p, 2, :, 0:COLS[2][p]] = weighted(p, 2).astype(BF)
        for i in range(2):
            side_sum(p, i).start()
    mine = []
    for p in (0, 2, 1):
        n = COLS[2][p]
        for i in range(2):
            total = weighted(p, 2 * i + 1)
            side_sum(p, i).wait_recv()
            added = total[i * 64:i * 64 + 64] + side[p, i, :, 0:n].astype(F32)
            t_tok[p, 2 * i + 1, i * 64:i * 64 + 64, 0:n] = added.astype(BF)
            t_tok[p, 2 * i + 1, 64 - i * 64:128 - i * 64, 0:n] = total[64 - i * 64:128 - i * 64].astype(BF)
            last_sum(p, i).start()
    for p in (0, 2, 1):
        n = COLS[2][p]
        t_tok[p, 0, :, 0:n] = weighted(p, 0).astype(BF)
        copy = pltpu.make_async_copy(t_tok.at[p, 0, :, pl.ds(0, n)], part.at[0, :, pl.ds(OFF[2][p], n)], lsem.at[p])
        copy.start()
        mine.append(copy)
    pair.wait()
    grad[...] = acc[0:1, :] + grecv[0:1, :]
    for p in range(3):
        sent(2, p)
        for k in range(3):
            relayed(k, p)
    for copy in mine:
        copy.wait()
    for p in range(3):
        for i in range(2):
            side_sum(p, i).wait_send()
            last_sum(p, i).wait()


def shards(tokens, expert_ids, route_weights, cotangent, w_gate, w_up, w_down, ia3_scale):
    owners = 64
    ids_t = expert_ids.T
    weights_t = route_weights.T.astype(F32)
    hit = ids_t[:, None, :] == jnp.arange(owners, dtype=jnp.int32)[None, :, None]
    chosen = jnp.sum(hit.astype(F32), axis=0)
    weight = jnp.sum(jnp.where(hit, weights_t[:, None, :], 0.0), axis=0)
    earlier = jnp.arange(TOK)[:, None] < jnp.arange(TOK)[None, :]
    rank = jnp.dot(chosen.astype(BF), earlier.astype(BF), preferred_element_type=F32)
    code = jnp.where(chosen > 0, rank, 99.0)
    both = jnp.stack([code, weight]).reshape(2, 4, 4, 4, TOK)
    cc = jnp.stack([
        both.transpose(1, 0, 2, 3, 4).reshape(4, 2, 16, TOK),
        both.transpose(2, 0, 3, 1, 4).reshape(4, 2, 16, TOK),
        both.transpose(3, 0, 1, 2, 4).reshape(4, 2, 16, TOK),
    ])
    hbm = pl.BlockSpec(memory_space=pl.ANY)
    vmem = pl.BlockSpec(memory_space=pltpu.VMEM)
    land = jax.ShapeDtypeStruct((3, PLANE, ROWS, WIDE), BF)
    dma = pltpu.SemaphoreType.DMA
    out = pl.pallas_call(
        kernel,
        out_shape=[jax.ShapeDtypeStruct((3, TOK, D), BF), jax.ShapeDtypeStruct((1, FF), F32), land, land, land,
                   jax.ShapeDtypeStruct((3, 3, 9, ROWS, WIDE), BF)],
        in_specs=[hbm] * 6 + [vmem],
        out_specs=[hbm, vmem, hbm, hbm, hbm, hbm],
        scratch_shapes=[
            pltpu.VMEM((3, SIDE, TOK, WIDE), BF),
            pltpu.VMEM((3, SIDE, TOK, WIDE), BF),
            pltpu.VMEM((3, PLANE, ROWS, WIDE), BF),
            pltpu.VMEM((3, PLANE, ROWS, WIDE), BF),
            pltpu.VMEM((PLANE, ROWS, WIDE), BF),
            pltpu.VMEM((3, SIDE, 2, PLANE, TOK), F32),
            pltpu.VMEM((D, FF), BF),
            pltpu.VMEM((D, FF), BF),
            pltpu.VMEM((FF, D), BF),
            pltpu.VMEM((1152, FF), F32),
            pltpu.VMEM((256, FF), BF),
            pltpu.VMEM((2, 256, D), BF),
            pltpu.VMEM((128, D), BF),
            pltpu.VMEM((3, 2, 64, WIDE), BF),
            pltpu.VMEM((3, SIDE, TOK, 384), BF),
            pltpu.VMEM((256, TOK), BF),
            pltpu.VMEM((8, FF), F32),
            pltpu.VMEM((8, FF), F32),
            pltpu.VMEM((8, FF), F32),
            dma((3,)), dma((9,)), dma((3, 3)), dma((3,)),
            dma((3, 3)), dma((3, 3)), dma((2, 3, 3)), dma((2, 3, 3)), dma((2, 3, 2)), dma((2, 3, 2)),
            dma((3, 3, PLANE)), dma((3, 3, PLANE)), dma((3, 3, 9)), dma((3, 3, 9)), dma((3, 2)), dma((3, 2)), dma((3, 2)), dma((3, 2)), dma(()), dma(()),
        ],
        compiler_params=pltpu.CompilerParams(collective_id=0, has_side_effects=True, vmem_limit_bytes=67043328),
    )(tokens, cotangent, cc, w_gate, w_up, w_down, ia3_scale)
    return jnp.sum(out[0].astype(F32), axis=0).astype(BF), out[1]


def solution(mesh):
    rows = P(("rep", "exp"), None)
    weights = P("exp", None, None)
    return jax.shard_map(
        shards, mesh=mesh, in_specs=(rows, rows, rows, rows, weights, weights, weights, P("exp", None)),
        out_specs=(rows, P("exp", None)), check_vma=False)
```
